256 devices in a mesh: segment: 16 (over z, x_lo), dp: 16 (over x_hi, y, core).
Axes of the slice: x: 4 (x_hi: 2, x_lo: 2; x = x_hi * 2 + x_lo), y: 4, z: 8, core: 2. Of those that a mesh axis runs over, the one named last changes fastest.
Arguments:
- checkpoint: bfloat16 [16, 2, 16, 16, 16, 1024], P('segment', None, 'dp'), may hold values from -6 to 6
- cotangent: bfloat16 [2, 16, 16, 16, 1024], P(None, 'dp'), may hold values from -6 to 6
- depthwise: float32 [16, 2, 25, 1024], P('segment'), may hold values from -1.8 to 1.8
- pointwise: bfloat16 [16, 1024, 2, 1024], P('segment', 'dp'), may hold values from -0.1875 to 0.1875
- genotype: int32 [16], P('segment'), may hold values from 0 to 2, as said below
Outputs:
- grad_input: bfloat16 [16, 2, 16, 16, 16, 1024], P('segment', None, 'dp')
- grad_point: float32 [16, 1024, 2, 1024], P('segment', 'dp')
- grad_depth: float32 [16, 2, 25, 1024], P('segment')
The draws below stay inside these ranges and needn't reach their ends.
Inputs may be any that keep to these rules, and one draw needn't show every extreme that they name: `genotype`: 0 separable 3x3, 1 separable 5x5, 2 dilated separable 3x3; both 0 and 2 occur.
All inputs are finite; a program needn't handle non-finite values.
Results may differ from the reference program's by a relative error of at most 0.025.
Values may be sent and summed in bfloat16 or wider, within the bound.
A program may use at most 128 MiB of HBM per device.

```python
import jax
import jax.numpy as jnp
from jax import lax

C = 1024
TAPS = 25
SIDE = 16
MICRO = 2
IMAGES = 16
SEGMENTS = 16


def draw_genotype(key, part):
    key_vals, key_first, key_second = jax.random.split(key, 3)
    values = jax.random.randint(key_vals, (SEGMENTS,), 0, 3)
    place_two = jax.random.randint(key_first, (), 0, SEGMENTS)
    place_zero = (place_two + 1 + jax.random.randint(key_second, (), 0, SEGMENTS - 1)) % SEGMENTS
    positions = jnp.arange(SEGMENTS)
    values = jnp.where(positions == place_two, 2, values)
    values = jnp.where(positions == place_zero, 0, values)
    return values.astype(jnp.int32)


def shard_levels(rng, dims, pieces, smallest, largest):
    def one(axis_at, shards_of):
        draws = jax.random.uniform(jax.random.fold_in(jax.random.fold_in(rng, 6), axis_at), (shards_of,), jnp.float32, smallest / len(pieces), largest / len(pieces))
        return jnp.repeat(jnp.exp(draws), dims[axis_at] // shards_of).reshape((-1,) + (1,) * (len(dims) - axis_at - 1))

    loudness = one(*pieces[0])
    for cut in pieces[1:]:
        loudness = loudness * one(*cut)
    return loudness


def scatter_about(key, shape, width, bound, cuts=(), held_as=jnp.bfloat16):
    array = jax.random.normal(key, shape, jnp.float32) * width
    if len(cuts) > 0:
        array = shard_levels(key, shape, cuts, -0.22, 0.18) * array
    return jnp.clip(array, min=-bound, max=bound).astype(held_as)


def setup_inputs(seed: int = 0) -> dict:
    seeds = jax.random.split(jax.random.key(seed), 6)
    return {
        "checkpoint": scatter_about(seeds[0], (SEGMENTS, MICRO, IMAGES, SIDE, SIDE, C), 1.0, 6.0, ((0, 16), (2, 16))),
        "cotangent": scatter_about(seeds[1], (MICRO, IMAGES, SIDE, SIDE, C), 1.0, 6.0, ((1, 16),)),
        "depthwise": scatter_about(seeds[2], (SEGMENTS, 2, TAPS, C), 0.3, 1.8, ((0, 16),), jnp.float32),
        "pointwise": scatter_about(seeds[3], (SEGMENTS, C, 2, C), C ** -0.5, 0.1875, ((0, 16), (1, 16))),
        "genotype": draw_genotype(jax.random.fold_in(seeds[5], 71), 0),
    }


def tap_mask(operation):
    tap_ids = jnp.arange(25, dtype=jnp.int32)
    row_off = tap_ids // 5 - 2
    col_off = tap_ids % 5 - 2
    narrow = (jnp.abs(row_off) <= 1) & (jnp.abs(col_off) <= 1)
    dilated = (row_off % 2 == 0) & (col_off % 2 == 0)
    kept_taps = jnp.where(operation == 0, narrow, jnp.where(operation == 1, True, dilated))
    return kept_taps.astype(jnp.float32)

def spread(values, kernel):
    grid_side = values.shape[1]
    padded = jnp.pad(values.astype(jnp.float32), ((0, 0), (2, 2), (2, 2), (0, 0)))
    running = jnp.zeros(values.shape, jnp.float32)
    for tap_number in range(25):
        tap_row, tap_col = divmod(tap_number, 5)
        running = running + kernel[tap_number] * padded[:, tap_row:tap_row + grid_side, tap_col:tap_col + grid_side, :]
    return running

def spread_back(gradient, kernel):
    grid_side = gradient.shape[1]
    padded = jnp.pad(gradient, ((0, 0), (2, 2), (2, 2), (0, 0)))
    running = jnp.zeros(gradient.shape, jnp.float32)
    for tap_number in range(25):
        tap_row, tap_col = divmod(tap_number, 5)
        running = running + kernel[tap_number] * padded[:, 4 - tap_row:4 - tap_row + grid_side, 4 - tap_col:4 - tap_col + grid_side, :]
    return running

def kernel_grad(values, gradient):
    grid_side = values.shape[1]
    padded = jnp.pad(values.astype(jnp.float32), ((0, 0), (2, 2), (2, 2), (0, 0)))
    columns = []
    for tap_number in range(25):
        tap_row, tap_col = divmod(tap_number, 5)
        window = padded[:, tap_row:tap_row + grid_side, tap_col:tap_col + grid_side, :]
        columns.append(lax.optimization_barrier(jnp.sum(window * gradient, axis=(0, 1, 2))))
    return jnp.stack(columns, 0)

def segment_backward(x_segment, upstream, depth_segment, panel, operation):
    tap_keep = tap_mask(operation)
    k_first = depth_segment[0] * tap_keep[:, None]
    k_second = depth_segment[1] * tap_keep[:, None]
    grid_shape = (MICRO * IMAGES, SIDE, SIDE, C)
    x_grid = x_segment.reshape(grid_shape)
    activated = jnp.maximum(x_grid, 0)
    first = spread(activated, k_first).astype(jnp.bfloat16)
    first_flat = first.reshape(-1, C)
    pre_act = jnp.dot(first_flat, panel[:, 0, :], preferred_element_type=jnp.float32)
    hidden = jax.nn.silu(pre_act).astype(jnp.bfloat16)
    mixed = spread(hidden.reshape(grid_shape), k_second).astype(jnp.bfloat16)
    up_flat = upstream.reshape(-1, C)
    grad_mix = jnp.dot(up_flat, panel[:, 1, :].T, preferred_element_type=jnp.float32)
    sigma = jax.nn.sigmoid(pre_act)
    slope = sigma * (1.0 + pre_act * (1.0 - sigma))
    grad_pre = (spread_back(grad_mix.reshape(grid_shape), k_second).reshape(-1, C) * slope).astype(jnp.bfloat16)
    grad_lin = jnp.dot(grad_pre, panel[:, 0, :].T, preferred_element_type=jnp.float32)
    grad_in = (upstream.reshape(grid_shape).astype(jnp.float32) + spread_back(grad_lin.reshape(grid_shape), k_first) * (x_grid > 0)).astype(jnp.bfloat16)
    w_grad = jnp.stack([jnp.dot(first_flat.T, grad_pre, preferred_element_type=jnp.float32), jnp.dot(mixed.reshape(-1, C).T, up_flat, preferred_element_type=jnp.float32)], 1)
    k_grad = jnp.stack([kernel_grad(activated, grad_lin.reshape(grid_shape)) * tap_keep[:, None], kernel_grad(hidden.reshape(grid_shape), grad_mix.reshape(grid_shape)) * tap_keep[:, None]], 0)
    return (grad_in.reshape(upstream.shape), w_grad, k_grad)

def reference(checkpoint, cotangent, depthwise, pointwise, genotype):
    mean_scale = 1.0 / (MICRO * IMAGES)

    def carried(upstream, segment_pack):
        x_segment, depth_segment, panel, operation = segment_pack
        grad_in, w_grad, k_grad = segment_backward(x_segment, upstream, depth_segment, panel, operation)
        return (grad_in, (grad_in, w_grad * mean_scale, k_grad * mean_scale))
    unused, outputs = lax.scan(carried, cotangent, (checkpoint, depthwise, pointwise, genotype), reverse=True)
    return (outputs[0], outputs[1], outputs[2])
```

```python
import jax
import jax.numpy as jnp
from jax import lax
from jax.experimental import pallas as pl
from jax.experimental.pallas import tpu as pltpu
from jax.sharding import PartitionSpec as P

BF = jnp.bfloat16
F32 = jnp.float32
MESH = pl.DeviceIdType.MESH
PIX = 256
CH = 1024
ROW = 160
PADDED = 20 * ROW
SCALE = 1.0 / 32


def tap_mask(operation):
    tap_ids = jnp.arange(25, dtype=jnp.int32)
    row_off = tap_ids // 5 - 2
    col_off = tap_ids % 5 - 2
    narrow = (jnp.abs(row_off) <= 1) & (jnp.abs(col_off) <= 1)
    dilated = (row_off % 2 == 0) & (col_off % 2 == 0)
    kept_taps = jnp.where(operation == 0, narrow, jnp.where(operation == 1, True, dilated))
    return kept_taps.astype(F32)


def dot_nn(a, b):
    return lax.dot_general(a, b, (((1,), (0,)), ((), ())), preferred_element_type=F32)


def dot_nt(a, b):
    return lax.dot_general(a, b, (((1,), (1,)), ((), ())), preferred_element_type=F32)


def dot_tn(a, b):
    return lax.dot_general(a, b, (((0,), (0,)), ((), ())), preferred_element_type=F32)


def kernel(
    x_hbm, cot_hbm, w_hbm, kk_hbm,
    dx_out, gp_out, gd_out,
    wb, pb, xb, kkb, apad, epad, gpad, bpad, cv, slope, bb, fb, dcb, dyb, dxr,
    r0, ra1, ra2, sa1, sa2, rb1, rb2, sb1, sb2,
    kgf, kgs, kgc, kgt, kgy, kgu, kgx, kgv, kgw,
    ls, ss, rs, turn,
):
    seg = lax.axis_index("segment")
    dp = lax.axis_index("dp")
    z, xl = lax.div(seg, 2), lax.rem(seg, 2)
    xh, y, c = lax.div(dp, 8), lax.rem(lax.div(dp, 2), 4), lax.rem(dp, 2)
    x = xh * 2 + xl
    home = 1 - xl
    mine = 1 - xl

    def at(x_, y_, z_, c_):
        return (z_ * 2 + lax.rem(x_, 2), lax.div(x_, 2) * 8 + y_ * 2 + c_)

    def turn4(v, by):
        return lax.rem(v + by, 4)

    x1, x2, x3 = turn4(x, 1), turn4(x, 2), turn4(x, 3)
    y1, y2, y3 = turn4(y, 1), turn4(y, 2), turn4(y, 3)
    right, far_x, left = at(x1, y, z, c), at(x2, y, z, c), at(x3, y, z, c)
    up, far_y, down = at(x, y1, z, c), at(x, y2, z, c), at(x, y3, z, c)
    sibling = at(x, y, z, 1 - c)
    partner = at(xh * 2 + 1 - xl, y, z, c)
    ahead = at(x, y, lax.rem(z + 7, 8), c)
    behind = at(x, y, lax.rem(z + 1, 8), c)

    def remote(src, dst, k, device):
        return pltpu.make_async_remote_copy(
            src_ref=src, dst_ref=dst, send_sem=ss.at[k], recv_sem=rs.at[k],
            device_id=device, device_id_type=MESH,
        )

    def local(src, dst, k):
        return pltpu.make_async_copy(src, dst, ls.at[k])

    barrier = pltpu.get_barrier_semaphore()
    greeted = (right, far_x, left, up, far_y, down, sibling, ahead, behind)
    for device in greeted:
        pl.semaphore_signal(barrier, inc=1, device_id=device, device_id_type=MESH)

    loads = [
        local(w_hbm, wb.at[home, :, xh, y, c], 0),
        local(x_hbm.at[mine], xb.at[home], 1),
        local(kk_hbm, kkb.at[home], 2),
    ]
    for load in loads:
        load.start()

    @pl.loop(0, 20)
    def _(r):
        nothing = jnp.zeros((ROW, 128), F32)
        for pad in (apad, epad, gpad, bpad):
            for i in range(2):
                pad[i, pl.ds(r * ROW, ROW), :] = nothing

    pl.semaphore_wait(barrier, len(greeted))

    for load in loads:
        load.wait()
    sent = []

    def go(src, dst, k, device):
        copy = remote(src, dst, k, device)
        copy.start()
        sent.append(copy)
        return copy

    def place_x(r):
        return 1 - lax.rem(r, 2), lax.div(r, 2)

    def ya(r, lo=0, n=64):
        return wb.at[home, 0, xh, r, c, pl.ds(lo, n)]

    def xa(r, lo=0, n=4):
        s, h = place_x(r)
        return wb.at[s, 0, h, pl.ds(lo, n), c]

    def xbk(r, lo=0, n=64):
        s, h = place_x(r)
        return wb.at[s, 1, h, y, c, pl.ds(lo, n)]

    def ybk(r, lo=0, n=2):
        return wb.at[pl.ds(lo, n), 1, :, r, c]

    a1p = go(ya(y), ya(y), 0, up)
    a1m = go(ya(y), ya(y), 1, down)
    b1p = go(xbk(x), xbk(x), 2, right)
    b1m = go(xbk(x), xbk(x), 3, left)
    kx = go(kk_hbm, kkb.at[home], 4, partner)
    xx = go(x_hbm.at[xl], xb.at[home], 5, partner)

    def to_pixels(pad, i, g, v):
        for p in range(16):
            pad[i, pl.ds((p + 2) * ROW + 16 + g, 16, stride=8), :] = v[p * 16 : p * 16 + 16]

    def spread_activation(i):
        for g in range(8):
            v = jnp.maximum(xb[i, :, g * 128 : g * 128 + 128].astype(F32), 0.0)
            to_pixels(apad, i, g, v)

    def conv(pad, i, which, flip):
        def step(p, _):
            acc = jnp.zeros((16, 8, 128), F32)
            for a in range(5):
                off = 4 - a if flip else a
                line = pad[i, pl.ds((p + off) * ROW, ROW), :].reshape(20, 8, 128)
                for b in range(5):
                    q = 4 - b if flip else b
                    tap = kkb[i, which, pl.ds((a * 5 + b) * 8, 8), :]
                    acc = acc + line[q : q + 16] * tap[None]
            cv[pl.ds(p * 128, 128), :] = acc.reshape(128, 128)
            return 0

        lax.fori_loop(0, 16, step, 0)

    def column(g):
        return cv[pl.ds(g, PIX, stride=8), :]

    a1p.wait_recv()
    a1q = go(ya(y3, 0, 32), ya(y3, 0, 32), 6, up)
    a1m.wait_recv()
    a1n = go(ya(y1, 32, 32), ya(y1, 32, 32), 7, down)
    b1p.wait_recv()
    b1q = go(xbk(x3, 0, 32), xbk(x3, 0, 32), 8, right)
    b1m.wait_recv()
    b1n = go(xbk(x1, 32, 32), xbk(x1, 32, 32), 9, left)
    a1q.wait_recv()
    a1n.wait_recv()
    a2p = go(xa(x), xa(x), 10, right)
    a2m = go(xa(x), xa(x), 11, left)
    b1q.wait_recv()
    b1n.wait_recv()
    b2p = go(ybk(y), ybk(y), 12, up)
    b2m = go(ybk(y), ybk(y), 13, down)
    fa0 = go(xa(x), xa(x), 14, sibling)
    fb0 = go(ybk(y), ybk(y), 15, sibling)

    kx.wait_recv()
    xx.wait_recv()

    def first_part(i, _):
        spread_activation(i)
        conv(apad, i, 0, False)
        for g in range(8):
            bb[i, :, g * 128 : g * 128 + 128] = column(g).astype(BF)
        return 0

    lax.fori_loop(0, 2, first_part, 0)

    a2p.wait_recv()
    a2q = go(xa(x3, 0, 2), xa(x3, 0, 2), 16, right)
    a2m.wait_recv()
    a2n = go(xa(x1, 2, 2), xa(x1, 2, 2), 17, left)
    b2p.wait_recv()
    b2q = go(ybk(y3, 0, 1), ybk(y3, 0, 1), 18, up)
    b2m.wait_recv()
    b2n = go(ybk(y1, 1, 1), ybk(y1, 1, 1), 19, down)
    fa1 = go(xa(x3), xa(x3), 20, sibling)
    fa2 = go(xa(x1), xa(x1), 21, sibling)
    fb1 = go(ybk(y3), ybk(y3), 22, sibling)
    fb2 = go(ybk(y1), ybk(y1), 23, sibling)
    a2q.wait_recv()
    a2n.wait_recv()
    fa3 = go(xa(x2), xa(x2), 24, sibling)
    b2q.wait_recv()
    b2n.wait_recv()
    fb3 = go(ybk(y2), ybk(y2), 25, sibling)
    for copy in (fa0, fa1, fa2, fa3):
        copy.wait_recv()

    def second_part(i, _):
        for n in range(4):
            pre = dot_nn(bb[i], wb[i, 0, :, :, :, :, n * 256 : n * 256 + 256].reshape(CH, 256))
            sg = 1.0 / (1.0 + jnp.exp(-pre))
            slope[i, :, n * 256 : n * 256 + 256] = sg * (1.0 + pre * (1.0 - sg))
            hidden = (pre * sg).astype(BF).astype(F32)
            for g in range(2):
                to_pixels(epad, i, n * 2 + g, hidden[:, g * 128 : g * 128 + 128])
        return 0

    lax.fori_loop(0, 2, second_part, 0)

    def third_part(i, _):
        conv(epad, i, 1, False)
        for g in range(8):
            fb[i, :, g * 128 : g * 128 + 128] = column(g).astype(BF)
        return 0

    @pl.when(z < 7)
    def _():
        lax.fori_loop(0, 2, third_part, 0)

    for copy in (fb0, fb1, fb2, fb3):
        copy.wait_recv()

    hop = remote(dyb.at[2], dyb.at[0], 26, ahead)

    @pl.when(z == 7)
    def _():
        load = local(cot_hbm.at[mine], dyb.at[0], 3)
        load.start()
        load.wait()

    @pl.when(z < 7)
    def _():
        hop.wait_recv()

    def stage(i, _):
        def rows(which, n):
            return wb[i, which, lax.div(n, 2), pl.ds(lax.rem(n, 2) * 2, 2)].reshape(256, CH)

        for n in range(4):
            gf = dot_nt(dyb[i], wb[i, 1, n // 2, pl.ds((n % 2) * 2, 2)].reshape(256, CH))
            for g in range(2):
                to_pixels(gpad, i, n * 2 + g, gf[:, g * 128 : g * 128 + 128])
        conv(gpad, i, 1, True)
        for g in range(8):
            cols = slice(g * 128, g * 128 + 128)
            dcb[i, :, cols] = (column(g) * slope[i, :, cols]).astype(BF)
        for n in range(4):
            gl = dot_nt(dcb[i], wb[i, 0, n // 2, pl.ds((n % 2) * 2, 2)].reshape(256, CH))
            for g in range(2):
                to_pixels(bpad, i, n * 2 + g, gl[:, g * 128 : g * 128 + 128])
        conv(bpad, i, 0, True)
        for g in range(8):
            cols = slice(g * 128, g * 128 + 128)
            kept = jnp.where(xb[i, :, cols].astype(F32) > 0, column(g), 0.0)
            dyb[i + 1, :, cols] = (dyb[i, :, cols].astype(F32) + kept).astype(BF)
        return 0

    lax.fori_loop(0, 2, stage, 0)

    @pl.when(z > 0)
    def _():
        @pl.when((z == 7) & (c == 1))
        def _():
            pl.semaphore_wait(turn, 1)

        hop.start()

        @pl.when((z == 7) & (c == 0))
        def _():
            hop.wait_send()
            pl.semaphore_signal(turn, inc=1, device_id=sibling, device_id_type=MESH)

    back = go(dyb.at[1 + xl], dxr, 27, partner)

    @pl.when(z == 7)
    def _():
        lax.fori_loop(0, 2, third_part, 0)

    def weigh(i, _):
        for n in range(4):
            cols = slice(n * 256, n * 256 + 256)
            first = dot_tn(bb[i, :, cols], dcb[i])
            pb[i, 0, n // 2, pl.ds((n % 2) * 2, 2)] = first.astype(BF).reshape(2, 2, 64, CH)
            second = dot_tn(fb[i, :, cols], dyb[i])
            pb[i, 1, n // 2, pl.ds((n % 2) * 2, 2)] = second.astype(BF).reshape(2, 2, 64, CH)
        return 0

    lax.fori_loop(0, 2, weigh, 0)

    c0 = go(pb.at[:, 0, :, :, 1 - c], r0.at[0], 28, sibling)
    c1 = go(pb.at[:, 1, :, :, 1 - c], r0.at[1], 29, sibling)

    def tap_sums(i, which, vpad, tpad):
        def step(p, totals):
            grad = tpad[i, pl.ds((p + 2) * ROW + 16, 128), :].reshape(16, 8, 128)
            out = []
            for a in range(5):
                line = vpad[i, pl.ds((p + a) * ROW, ROW), :].reshape(20, 8, 128)
                for b in range(5):
                    out.append(totals[a * 5 + b] + jnp.sum(line[b : b + 16] * grad, axis=0))
            return tuple(out)

        totals = lax.fori_loop(0, 16, step, tuple(jnp.zeros((8, 128), F32) for _ in range(25)))
        for t in range(25):
            kgf[i, pl.ds(which * 200 + t * 8, 8), :] = totals[t]

    def taps(i, _):
        tap_sums(i, 0, apad, bpad)
        tap_sums(i, 1, epad, gpad)
        return 0

    lax.fori_loop(0, 2, taps, 0)
    kgs[...] = kgf[1 - c].astype(BF)
    k0 = go(kgs, kgc, 30, sibling)

    def add_first(which, copy):
        copy.wait_recv()

        def step(b, _):
            s, h, r = lax.div(b, 8), lax.rem(lax.div(b, 4), 2), lax.rem(b, 4)
            total = pb[s, which, h, r, c].astype(F32) + r0[which, s, h, r].astype(F32)
            pb[s, which, h, r, c] = total.astype(BF)
            return 0

        lax.fori_loop(0, 16, step, 0)

    def gya(r, lo=0, n=2):
        return pb.at[pl.ds(lo, n), 0, :, r, c]

    def gxb(r, lo=0, n=4):
        s, h = place_x(r)
        return pb.at[s, 1, h, pl.ds(lo, n), c]

    def gxa(r, lo=0, n=64):
        s, h = place_x(r)
        return pb.at[s, 0, h, y, c, pl.ds(lo, n)]

    def gyb(r, lo=0, n=64):
        return pb.at[home, 1, xh, r, c, pl.ds(lo, n)]

    def plus(ref, *others):
        total = ref[...].astype(F32)
        for other in others:
            total = total + other[...].astype(F32)
        return total

    add_first(0, c0)
    d1p = go(gya(y2, 0, 1), ra1.at[0], 31, up)
    d1m = go(gya(y2, 1, 1), ra1.at[1], 32, down)
    add_first(1, c1)
    e1p = go(gxb(x2, 0, 2), rb1.at[0], 33, right)
    e1m = go(gxb(x2, 2, 2), rb1.at[1], 34, left)
    k0.wait_recv()
    kgt[...] = (kgf[c] + kgc[...].astype(F32)).astype(BF)
    ky = [go(kgt, kgy.at[j], 35 + j, device) for j, device in enumerate((up, far_y, down))]

    d1p.wait_recv()
    gya(y1, 0, 1)[...] = plus(gya(y1, 0, 1), ra1.at[0]).astype(BF)
    d2p = go(gya(y1), ra2.at[0], 38, up)
    d1m.wait_recv()
    gya(y3, 1, 1)[...] = plus(gya(y3, 1, 1), ra1.at[1]).astype(BF)
    d2m = go(gya(y3), ra2.at[1], 39, down)
    e1p.wait_recv()
    gxb(x1, 0, 2)[...] = plus(gxb(x1, 0, 2), rb1.at[0]).astype(BF)
    e2p = go(gxb(x1), rb2.at[0], 40, right)
    e1m.wait_recv()
    gxb(x3, 2, 2)[...] = plus(gxb(x3, 2, 2), rb1.at[1]).astype(BF)
    e2m = go(gxb(x3), rb2.at[1], 41, left)

    for copy in ky:
        copy.wait_recv()
    kgu[...] = plus(kgt, kgy.at[0], kgy.at[1], kgy.at[2]).astype(BF)
    kq = [go(kgu, kgx.at[j], 42 + j, device) for j, device in enumerate((right, far_x, left))]

    d2p.wait_recv()
    d2m.wait_recv()
    gya(y)[...] = plus(gya(y), ra2.at[0], ra2.at[1]).astype(BF)
    d3p = go(gxa(x2, 0, 32), sa1.at[0], 45, right)
    d3m = go(gxa(x2, 32, 32), sa1.at[1], 46, left)
    e2p.wait_recv()
    e2m.wait_recv()
    gxb(x)[...] = plus(gxb(x), rb2.at[0], rb2.at[1]).astype(BF)
    e3p = go(gyb(y2, 0, 32), sb1.at[0], 47, up)
    e3m = go(gyb(y2, 32, 32), sb1.at[1], 48, down)

    for copy in kq:
        copy.wait_recv()
    kgv[...] = plus(kgu, kgx.at[0], kgx.at[1], kgx.at[2]).astype(BF)
    k3 = go(kgv, kgw, 49, sibling)

    d3p.wait_recv()
    gxa(x1, 0, 32)[...] = plus(gxa(x1, 0, 32), sa1.at[0]).astype(BF)
    d4p = go(gxa(x1), sa2.at[0], 50, right)
    d3m.wait_recv()
    gxa(x3, 32, 32)[...] = plus(gxa(x3, 32, 32), sa1.at[1]).astype(BF)
    d4m = go(gxa(x3), sa2.at[1], 51, left)
    e3p.wait_recv()
    gyb(y1, 0, 32)[...] = plus(gyb(y1, 0, 32), sb1.at[0]).astype(BF)
    e4p = go(gyb(y1), sb2.at[0], 52, up)
    e3m.wait_recv()
    gyb(y3, 32, 32)[...] = plus(gyb(y3, 32, 32), sb1.at[1]).astype(BF)
    e4m = go(gyb(y3), sb2.at[1], 53, down)

    back.wait_recv()
    store0 = local(dyb.at[home + 1], dx_out.at[mine], 4)
    store1 = local(dxr, dx_out.at[1 - mine], 5)
    store0.start()
    store1.start()
    k3.wait_recv()
    own = (c == home).astype(F32)
    gd_out[...] = (kgv[...].astype(F32) * own + kgw[...].astype(F32) * (1.0 - own)) * SCALE

    d4p.wait_recv()
    d4m.wait_recv()
    gp_out[0] = plus(gxa(x), sa2.at[0], sa2.at[1]) * SCALE
    e4p.wait_recv()
    e4m.wait_recv()
    gp_out[1] = plus(gyb(y), sb2.at[0], sb2.at[1]) * SCALE

    store0.wait()
    store1.wait()
    for copy in sent:
        copy.wait_send()

    @pl.when((z > 0) & ((z < 7) | (c == 1)))
    def _():
        hop.wait_send()


def body(checkpoint, cotangent, depthwise, pointwise, genotype):
    x = checkpoint.reshape(2, PIX, CH)
    cot = cotangent.reshape(2, PIX, CH)
    keep = tap_mask(genotype[0])
    kk = (depthwise[0] * keep[None, :, None]).reshape(2, 200, 128)
    w = jnp.transpose(pointwise[0], (1, 0, 2))
    anywhere = pl.BlockSpec(memory_space=pl.ANY)
    here = pl.BlockSpec(memory_space=pltpu.VMEM)
    pad = pltpu.VMEM((2, PADDED, 128), F32)
    taps = pltpu.VMEM((400, 128), BF)
    image2 = pltpu.VMEM((2, PIX, CH), BF)
    dx, gp, gd = pl.pallas_call(
        kernel,
        out_shape=(
            jax.ShapeDtypeStruct((2, PIX, CH), BF),
            jax.ShapeDtypeStruct((2, 64, CH), F32),
            jax.ShapeDtypeStruct((400, 128), F32),
        ),
        in_specs=[anywhere] * 4,
        out_specs=(anywhere, here, here),
        scratch_shapes=[
            pltpu.VMEM((2, 2, 2, 4, 2, 64, CH), BF),
            pltpu.VMEM((2, 2, 2, 4, 2, 64, CH), BF),
            image2,
            pltpu.VMEM((2, 2, 200, 128), F32),
            pad, pad, pad, pad,
            pltpu.VMEM((PIX * 8, 128), F32),
            pltpu.VMEM((2, PIX, CH), F32),
            image2, image2, image2,
            pltpu.VMEM((3, PIX, CH), BF),
            pltpu.VMEM((PIX, CH), BF),
            pltpu.VMEM((2, 2, 2, 4, 64, CH), BF),
            pltpu.VMEM((2, 1, 2, 64, CH), BF),
            pltpu.VMEM((2, 2, 2, 64, CH), BF),
            pltpu.VMEM((2, 32, CH), BF),
            pltpu.VMEM((2, 64, CH), BF),
            pltpu.VMEM((2, 2, 64, CH), BF),
            pltpu.VMEM((2, 4, 64, CH), BF),
            pltpu.VMEM((2, 32, CH), BF),
            pltpu.VMEM((2, 64, CH), BF),
            pltpu.VMEM((2, 400, 128), F32),
            taps, taps, taps,
            pltpu.VMEM((3, 400, 128), BF),
            taps,
            pltpu.VMEM((3, 400, 128), BF),
            taps, taps,
            pltpu.SemaphoreType.DMA((6,)),
            pltpu.SemaphoreType.DMA((54,)),
            pltpu.SemaphoreType.DMA((54,)),
            pltpu.SemaphoreType.REGULAR,
        ],
        compiler_params=pltpu.CompilerParams(
            collective_id=0, has_side_effects=True, vmem_limit_bytes=66_000_000
        ),
    )(x, cot, w, kk)
    grad_depth = gd.reshape(2, 25, CH) * keep[None, :, None]
    return (
        dx.reshape(checkpoint.shape),
        jnp.transpose(gp, (1, 0, 2))[None],
        grad_depth[None],
    )


def solution(mesh):
    placed = (
        P("segment", None, "dp", None, None, None),
        P(None, "dp", None, None, None),
        P("segment", None, None, None),
        P("segment", "dp", None, None),
        P("segment"),
    )
    return jax.shard_map(
        body,
        mesh=mesh,
        in_specs=placed,
        out_specs=(
            P("segment", None, "dp", None, None, None),
            P("segment", "dp", None, None),
            P("segment", None, None, None),
        ),
        check_vma=False,
    )
```

```python
import jax
import jax.numpy as jnp
from jax import lax
from jax.experimental import pallas as pl
from jax.experimental.pallas import tpu as pltpu
from jax.sharding import PartitionSpec as P

BF = jnp.bfloat16
F32 = jnp.float32
MESH = pl.DeviceIdType.MESH
PIX = 256
CH = 1024
ROW = 160
PADDED = 20 * ROW
SCALE = 1.0 / 32


def tap_mask(operation):
    tap_ids = jnp.arange(25, dtype=jnp.int32)
    row_off = tap_ids // 5 - 2
    col_off = tap_ids % 5 - 2
    narrow = (jnp.abs(row_off) <= 1) & (jnp.abs(col_off) <= 1)
    dilated = (row_off % 2 == 0) & (col_off % 2 == 0)
    kept_taps = jnp.where(operation == 0, narrow, jnp.where(operation == 1, True, dilated))
    return kept_taps.astype(F32)


def dot_nn(a, b):
    return lax.dot_general(a, b, (((1,), (0,)), ((), ())), preferred_element_type=F32)


def dot_nt(a, b):
    return lax.dot_general(a, b, (((1,), (1,)), ((), ())), preferred_element_type=F32)


def dot_tn(a, b):
    return lax.dot_general(a, b, (((0,), (0,)), ((), ())), preferred_element_type=F32)


def kernel(
    x_hbm, cot_hbm, w_hbm, kk_hbm,
    dx_out, gp_out, gd_out,
    wb, pb, xb, kkb, apad, epad, gpad, bpad, slope, bb, fb, dcb, dyb, dxr,
    r0, ra1, ra2, sa1, sa2, rb1, rb2, sb1, sb2,
    kgf, kgs, kgc, kgt, kgy, kgu, kgx, kgv, kgw,
    ls, ss, rs, turn,
):
    seg = lax.axis_index("segment")
    dp = lax.axis_index("dp")
    z, xl = lax.div(seg, 2), lax.rem(seg, 2)
    xh, y, c = lax.div(dp, 8), lax.rem(lax.div(dp, 2), 4), lax.rem(dp, 2)
    x = xh * 2 + xl
    home = 1 - xl
    mine = 1 - xl

    def at(x_, y_, z_, c_):
        return (z_ * 2 + lax.rem(x_, 2), lax.div(x_, 2) * 8 + y_ * 2 + c_)

    def turn4(v, by):
        return lax.rem(v + by, 4)

    x1, x2, x3 = turn4(x, 1), turn4(x, 2), turn4(x, 3)
    y1, y2, y3 = turn4(y, 1), turn4(y, 2), turn4(y, 3)
    right, far_x, left = at(x1, y, z, c), at(x2, y, z, c), at(x3, y, z, c)
    up, far_y, down = at(x, y1, z, c), at(x, y2, z, c), at(x, y3, z, c)
    sibling = at(x, y, z, 1 - c)
    partner = at(xh * 2 + 1 - xl, y, z, c)
    ahead = at(x, y, lax.rem(z + 7, 8), c)
    behind = at(x, y, lax.rem(z + 1, 8), c)

    def remote(src, dst, k, device):
        return pltpu.make_async_remote_copy(
            src_ref=src, dst_ref=dst, send_sem=ss.at[k], recv_sem=rs.at[k],
            device_id=device, device_id_type=MESH,
        )

    def local(src, dst, k):
        return pltpu.make_async_copy(src, dst, ls.at[k])

    barrier = pltpu.get_barrier_semaphore()
    greeted = (right, far_x, left, up, far_y, down, sibling, ahead, behind)
    for device in greeted:
        pl.semaphore_signal(barrier, inc=1, device_id=device, device_id_type=MESH)

    loads = [
        local(w_hbm, wb.at[home, :, xh, y, c], 0),
        local(x_hbm.at[mine], xb.at[home], 1),
        local(kk_hbm, kkb.at[home], 2),
    ]
    for load in loads:
        load.start()

    @pl.loop(0, 20)
    def _(r):
        nothing = jnp.zeros((ROW, 128), F32)
        for pad in (apad, epad, gpad, bpad):
            for i in range(2):
                pad[i, pl.ds(r * ROW, ROW), :] = nothing

    pl.semaphore_wait(barrier, len(greeted))

    for load in loads:
        load.wait()
    sent = []

    def go(src, dst, k, device):
        copy = remote(src, dst, k, device)
        copy.start()
        sent.append(copy)
        return copy

    def place_x(r):
        return 1 - lax.rem(r, 2), lax.div(r, 2)

    def ya(r, lo=0, n=64):
        return wb.at[home, 0, xh, r, c, pl.ds(lo, n)]

    def xa(r, lo=0, n=4):
        s, h = place_x(r)
        return wb.at[s, 0, h, pl.ds(lo, n), c]

    def xbk(r, lo=0, n=64):
        s, h = place_x(r)
        return wb.at[s, 1, h, y, c, pl.ds(lo, n)]

    def ybk(r, lo=0, n=2):
        return wb.at[pl.ds(lo, n), 1, :, r, c]

    a1p = go(ya(y), ya(y), 0, up)
    a1m = go(ya(y), ya(y), 1, down)
    b1p = go(xbk(x), xbk(x), 2, right)
    b1m = go(xbk(x), xbk(x), 3, left)
    kx = go(kk_hbm, kkb.at[home], 4, partner)

    def to_pixels(pad, i, g, v, row=0):
        for p in range(v.shape[0] // 16):
            start = (p + row + 2) * ROW + 16 + g
            pad[i, pl.ds(start, 16, stride=8), :] = v[p * 16 : p * 16 + 16]

    def spread_activation(i):
        for g in range(8):
            v = jnp.maximum(xb[i, :, g * 128 : g * 128 + 128].astype(F32), 0.0)
            to_pixels(apad, i, g, v)

    def conv(pad, i, which, flip, lo, hi, finish):
        def step(p, _):
            acc = jnp.zeros((16, 8, 128), F32)
            for a in range(5):
                off = 4 - a if flip else a
                line = pad[i, pl.ds((p + off) * ROW, ROW), :].reshape(20, 8, 128)
                for b in range(5):
                    q = 4 - b if flip else b
                    tap = kkb[i, which, pl.ds((a * 5 + b) * 8, 8), :]
                    acc = acc + line[q : q + 16] * tap[None]
            by_group = jnp.swapaxes(acc, 0, 1)
            here = pl.ds(pl.multiple_of(p * 16, 16), 16)
            for g in range(8):
                finish(here, slice(g * 128, g * 128 + 128), by_group[g])
            return 0

        lax.fori_loop(lo, hi, step, 0)

    def rounded_to(ref, i):
        def finish(here, cols, v):
            ref[i, here, cols] = v.astype(BF)

        return finish

    def first_part(i):
        spread_activation(i)
        conv(apad, i, 0, False, 0, 16, rounded_to(bb, i))

    def second_part(i):
        for n in range(4):
            pre = dot_nn(bb[i], wb[i, 0, :, :, :, :, n * 256 : n * 256 + 256].reshape(CH, 256))
            sg = 1.0 / (1.0 + jnp.exp(-pre))
            slope[i, :, n * 256 : n * 256 + 256] = sg * (1.0 + pre * (1.0 - sg))
            hidden = (pre * sg).astype(BF).astype(F32)
            for g in range(2):
                to_pixels(epad, i, n * 2 + g, hidden[:, g * 128 : g * 128 + 128])

    a1p.wait_recv()
    a1q = go(ya(y3, 0, 32), ya(y3, 0, 32), 6, up)
    a1m.wait_recv()
    a1n = go(ya(y1, 32, 32), ya(y1, 32, 32), 7, down)
    b1p.wait_recv()
    b1q = go(xbk(x3, 0, 32), xbk(x3, 0, 32), 8, right)
    b1m.wait_recv()
    b1n = go(xbk(x1, 32, 32), xbk(x1, 32, 32), 9, left)
    a1q.wait_recv()
    a1n.wait_recv()
    a2p = go(xa(x), xa(x), 10, right)
    a2m = go(xa(x), xa(x), 11, left)
    b1q.wait_recv()
    b1n.wait_recv()
    b2p = go(ybk(y), ybk(y), 12, up)
    b2m = go(ybk(y), ybk(y), 13, down)
    xx = go(x_hbm.at[xl], xb.at[home], 5, partner)
    fa0 = go(xa(x), xa(x), 14, sibling)
    fb0 = go(ybk(y), ybk(y), 15, sibling)

    first_part(home)

    a2p.wait_recv()
    a2q = go(xa(x3), xa(x3), 16, right)
    b2p.wait_recv()
    b2q = go(ybk(y3, 0, 1), ybk(y3, 0, 1), 18, up)
    b2m.wait_recv()
    b2n = go(ybk(y1, 1, 1), ybk(y1, 1, 1), 19, down)
    a2m.wait_recv()
    fa1 = go(xa(x3), xa(x3), 20, sibling)
    fa2 = go(xa(x1), xa(x1), 21, sibling)
    fb1 = go(ybk(y3), ybk(y3), 22, sibling)
    fb2 = go(ybk(y1), ybk(y1), 23, sibling)

    kx.wait_recv()
    xx.wait_recv()
    first_part(1 - home)

    a2q.wait_recv()
    fa3 = go(xa(x2), xa(x2), 24, sibling)
    b2q.wait_recv()
    b2n.wait_recv()
    fb3 = go(ybk(y2), ybk(y2), 25, sibling)
    for copy in (fa0, fa1, fa2, fa3):
        copy.wait_recv()
    second_part(0)

    def third_part(i, _):
        conv(epad, i, 1, False, 0, 16, rounded_to(fb, i))
        return 0

    @pl.when(z < 7)
    def _():
        second_part(1)
        lax.fori_loop(0, 2, third_part, 0)

    for copy in (fb0, fb1, fb2, fb3):
        copy.wait_recv()

    hops = [
        remote(dyb.at[2, pl.ds(k * 64, 64)], dyb.at[0, pl.ds(k * 64, 64)], (26, 54, 55, 56)[k], ahead)
        for k in range(4)
    ]

    @pl.when(z == 7)
    def _():
        load = local(cot_hbm.at[mine], dyb.at[0], 3)
        load.start()
        load.wait()

    def grad_mix(i, lo, n_rows):
        for n in range(4):
            gf = dot_nt(
                dyb[i, pl.ds(lo * 16, n_rows * 16)],
                wb[i, 1, n // 2, pl.ds((n % 2) * 2, 2)].reshape(256, CH),
            )
            for g in range(2):
                to_pixels(gpad, i, n * 2 + g, gf[:, g * 128 : g * 128 + 128], lo)

    def grad_lin(i):
        for n in range(4):
            gl = dot_nt(dcb[i], wb[i, 0, n // 2, pl.ds((n % 2) * 2, 2)].reshape(256, CH))
            for g in range(2):
                to_pixels(bpad, i, n * 2 + g, gl[:, g * 128 : g * 128 + 128])

    def through_slope(i):
        def finish(here, cols, v):
            dcb[i, here, cols] = (v * slope[i, here, cols]).astype(BF)

        return finish

    def onto_input(i):
        def finish(here, cols, v):
            kept = jnp.where(xb[i, here, cols].astype(F32) > 0, v, 0.0)
            dyb[i + 1, here, cols] = (dyb[i, here, cols].astype(F32) + kept).astype(BF)

        return finish

    done = 0
    for k, ready in enumerate((0, 6, 10, 16)):
        @pl.when(z < 7)
        def _():
            hops[k].wait_recv()

        grad_mix(0, k * 4, 4)
        if ready > done:
            conv(gpad, 0, 1, True, done, ready, through_slope(0))
        done = ready
    grad_lin(0)
    conv(bpad, 0, 0, True, 0, 16, onto_input(0))

    @pl.when(z == 7)
    def _():
        second_part(1)

    grad_mix(1, 0, 16)
    conv(gpad, 1, 1, True, 0, 16, through_slope(1))
    grad_lin(1)
    for k in range(4):
        conv(bpad, 1, 0, True, k * 4, k * 4 + 4, onto_input(1))

        @pl.when(z > 0)
        def _():
            if k == 0:
                @pl.when((z == 7) & (c == 1))
                def _():
                    pl.semaphore_wait(turn, 1)

            hops[k].start()

    @pl.when((z == 7) & (c == 0))
    def _():
        for hop in hops:
            hop.wait_send()
        pl.semaphore_signal(turn, inc=1, device_id=sibling, device_id_type=MESH)

    back = go(dyb.at[1 + xl], dxr, 27, partner)

    @pl.when(z == 7)
    def _():
        lax.fori_loop(0, 2, third_part, 0)

    def weigh(i, _):
        for n in range(4):
            cols = slice(n * 256, n * 256 + 256)
            first = dot_tn(bb[i, :, cols], dcb[i])
            pb[i, 0, n // 2, pl.ds((n % 2) * 2, 2)] = first.astype(BF).reshape(2, 2, 64, CH)
            second = dot_tn(fb[i, :, cols], dyb[i])
            pb[i, 1, n // 2, pl.ds((n % 2) * 2, 2)] = second.astype(BF).reshape(2, 2, 64, CH)
        return 0

    lax.fori_loop(0, 2, weigh, 0)

    def tap_sums(i, which, vpad, tpad):
        def step(p, totals):
            grad = tpad[i, pl.ds((p + 2) * ROW + 16, 128), :].reshape(16, 8, 128)
            out = []
            for a in range(5):
                line = vpad[i, pl.ds((p + a) * ROW, ROW), :].reshape(20, 8, 128)
                for b in range(5):
                    out.append(totals[a * 5 + b] + jnp.sum(line[b : b + 16] * grad, axis=0))
            return tuple(out)

        totals = lax.fori_loop(0, 16, step, tuple(jnp.zeros((8, 128), F32) for _ in range(25)))
        for t in range(25):
            kgf[i, pl.ds(which * 200 + t * 8, 8), :] = totals[t]

    def gya(r, core, lo=0, n=2):
        return pb.at[pl.ds(lo, n), 0, :, r, core]

    def gxb(r, core, lo=0, n=4):
        s, h = place_x(r)
        return pb.at[s, 1, h, pl.ds(lo, n), core]

    def gxa(r, lo=0, n=64):
        s, h = place_x(r)
        return pb.at[s, 0, h, y, c, pl.ds(lo, n)]

    def gyb(r, lo=0, n=64):
        return pb.at[home, 1, xh, r, c, pl.ds(lo, n)]

    def r0a(r):
        return r0.at[0, :, :, r]

    def r0b(r):
        s, h = place_x(r)
        return r0.at[1, s, h]

    def plus(ref, *others):
        total = ref[...].astype(F32)
        for other in others:
            total = total + other[...].astype(F32)
        return total

    pair_a = {}
    pair_b = {}
    for n, (ry, rx) in enumerate(((y2, x2), (y1, x1), (y3, x3), (y, x))):
        pair_a[n] = go(gya(ry, 1 - c), r0a(ry), 57 + n, sibling)
        pair_b[n] = go(gxb(rx, 1 - c), r0b(rx), 61 + n, sibling)

    def merge_a(n, r):
        pair_a[n].wait_recv()
        ref = gya(r, c)
        ref[...] = plus(ref, r0a(r)).astype(BF)

    def merge_b(n, r):
        pair_b[n].wait_recv()
        ref = gxb(r, c)
        ref[...] = plus(ref, r0b(r)).astype(BF)

    merge_a(0, y2)
    d1p = go(gya(y2, c, 0, 1), ra1.at[0], 31, up)
    d1m = go(gya(y2, c, 1, 1), ra1.at[1], 32, down)
    merge_b(0, x2)
    e1p = go(gxb(x2, c, 0, 2), rb1.at[0], 33, right)
    e1m = go(gxb(x2, c, 2, 2), rb1.at[1], 34, left)
    merge_a(1, y1)
    d2p = [go(gya(y1, c, 1, 1), ra2.at[0, 1:2], 38, up)]
    merge_a(2, y3)
    d2m = [go(gya(y3, c, 0, 1), ra2.at[1, 0:1], 39, down)]
    merge_b(1, x1)
    e2p = [go(gxb(x1, c, 2, 2), rb2.at[0, 2:4], 40, right)]
    merge_b(2, x3)
    e2m = [go(gxb(x3, c, 0, 2), rb2.at[1, 0:2], 41, left)]
    tap_sums(0, 0, apad, bpad)
    tap_sums(0, 1, epad, gpad)

    def pass_on(first, ref, arrived, dst, k, device):
        first.wait_recv()
        ref[...] = plus(ref, arrived).astype(BF)
        return go(ref, dst, k, device)

    d2p.append(pass_on(d1p, gya(y1, c, 0, 1), ra1.at[0], ra2.at[0, 0:1], 65, up))
    d2m.append(pass_on(d1m, gya(y3, c, 1, 1), ra1.at[1], ra2.at[1, 1:2], 66, down))
    e2p.append(pass_on(e1p, gxb(x1, c, 0, 2), rb1.at[0], rb2.at[0, 0:2], 67, right))
    e2m.append(pass_on(e1m, gxb(x3, c, 2, 2), rb1.at[1], rb2.at[1, 2:4], 68, left))
    merge_a(3, y)
    merge_b(3, x)
    tap_sums(1, 0, apad, bpad)
    tap_sums(1, 1, epad, gpad)
    kgs[...] = kgf[1 - c].astype(BF)
    k0 = go(kgs, kgc, 30, sibling)

    for copy in d2p + d2m:
        copy.wait_recv()
    gya(y, c)[...] = plus(gya(y, c), ra2.at[0], ra2.at[1]).astype(BF)
    d3p = go(gxa(x2, 0, 32), sa1.at[0], 45, right)
    d3m = go(gxa(x2, 32, 32), sa1.at[1], 46, left)
    d4p = [go(gxa(x1, 32, 32), sa2.at[0, 32:64], 50, right)]
    d4m = [go(gxa(x3, 0, 32), sa2.at[1, 0:32], 51, left)]
    for copy in e2p + e2m:
        copy.wait_recv()
    gxb(x, c)[...] = plus(gxb(x, c), rb2.at[0], rb2.at[1]).astype(BF)
    e3p = go(gyb(y2, 0, 32), sb1.at[0], 47, up)
    e3m = go(gyb(y2, 32, 32), sb1.at[1], 48, down)
    e4p = [go(gyb(y1, 32, 32), sb2.at[0, 32:64], 52, up)]
    e4m = [go(gyb(y3, 0, 32), sb2.at[1, 0:32], 53, down)]

    k0.wait_recv()
    kgt[...] = (kgf[c] + kgc[...].astype(F32)).astype(BF)
    ky = [go(kgt, kgy.at[j], 35 + j, device) for j, device in enumerate((up, far_y, down))]

    d4p.append(pass_on(d3p, gxa(x1, 0, 32), sa1.at[0], sa2.at[0, 0:32], 69, right))
    d4m.append(pass_on(d3m, gxa(x3, 32, 32), sa1.at[1], sa2.at[1, 32:64], 70, left))
    e4p.append(pass_on(e3p, gyb(y1, 0, 32), sb1.at[0], sb2.at[0, 0:32], 71, up))
    e4m.append(pass_on(e3m, gyb(y3, 32, 32), sb1.at[1], sb2.at[1, 32:64], 72, down))

    for copy in ky:
        copy.wait_recv()
    kgu[...] = plus(kgt, kgy.at[0], kgy.at[1], kgy.at[2]).astype(BF)
    kq = [go(kgu, kgx.at[j], 42 + j, device) for j, device in enumerate((right, far_x, left))]

    back.wait_recv()
    store0 = local(dyb.at[home + 1], dx_out.at[mine], 4)
    store1 = local(dxr, dx_out.at[1 - mine], 5)
    store0.start()
    store1.start()

    for copy in d4p + d4m:
        copy.wait_recv()
    gp_out[0] = plus(gxa(x), sa2.at[0], sa2.at[1]) * SCALE
    for copy in e4p + e4m:
        copy.wait_recv()
    gp_out[1] = plus(gyb(y), sb2.at[0], sb2.at[1]) * SCALE

    for copy in kq:
        copy.wait_recv()
    kgv[...] = plus(kgu, kgx.at[0], kgx.at[1], kgx.at[2]).astype(BF)
    k3 = go(kgv, kgw, 49, sibling)
    k3.wait_recv()
    own = (c == home).astype(F32)
    gd_out[...] = (kgv[...].astype(F32) * own + kgw[...].astype(F32) * (1.0 - own)) * SCALE

    store0.wait()
    store1.wait()
    for copy in sent:
        copy.wait_send()

    @pl.when((z > 0) & ((z < 7) | (c == 1)))
    def _():
        for hop in hops:
            hop.wait_send()


def body(checkpoint, cotangent, depthwise, pointwise, genotype):
    x = checkpoint.reshape(2, PIX, CH)
    cot = cotangent.reshape(2, PIX, CH)
    keep = tap_mask(genotype[0])
    kk = (depthwise[0] * keep[None, :, None]).reshape(2, 200, 128)
    w = jnp.transpose(pointwise[0], (1, 0, 2))
    anywhere = pl.BlockSpec(memory_space=pl.ANY)
    here = pl.BlockSpec(memory_space=pltpu.VMEM)
    pad = pltpu.VMEM((2, PADDED, 128), F32)
    taps = pltpu.VMEM((400, 128), BF)
    image2 = pltpu.VMEM((2, PIX, CH), BF)
    dx, gp, gd = pl.pallas_call(
        kernel,
        out_shape=(
            jax.ShapeDtypeStruct((2, PIX, CH), BF),
            jax.ShapeDtypeStruct((2, 64, CH), F32),
            jax.ShapeDtypeStruct((400, 128), F32),
        ),
        in_specs=[anywhere] * 4,
        out_specs=(anywhere, here, here),
        scratch_shapes=[
            pltpu.VMEM((2, 2, 2, 4, 2, 64, CH), BF),
            pltpu.VMEM((2, 2, 2, 4, 2, 64, CH), BF),
            image2,
            pltpu.VMEM((2, 2, 200, 128), F32),
            pad, pad, pad, pad,
            pltpu.VMEM((2, PIX, CH), F32),
            image2, image2, image2,
            pltpu.VMEM((3, PIX, CH), BF),
            pltpu.VMEM((PIX, CH), BF),
            pltpu.VMEM((2, 2, 2, 4, 64, CH), BF),
            pltpu.VMEM((2, 1, 2, 64, CH), BF),
            pltpu.VMEM((2, 2, 2, 64, CH), BF),
            pltpu.VMEM((2, 32, CH), BF),
            pltpu.VMEM((2, 64, CH), BF),
            pltpu.VMEM((2, 2, 64, CH), BF),
            pltpu.VMEM((2, 4, 64, CH), BF),
            pltpu.VMEM((2, 32, CH), BF),
            pltpu.VMEM((2, 64, CH), BF),
            pltpu.VMEM((2, 400, 128), F32),
            taps, taps, taps,
            pltpu.VMEM((3, 400, 128), BF),
            taps,
            pltpu.VMEM((3, 400, 128), BF),
            taps, taps,
            pltpu.SemaphoreType.DMA((6,)),
            pltpu.SemaphoreType.DMA((73,)),
            pltpu.SemaphoreType.DMA((73,)),
            pltpu.SemaphoreType.REGULAR,
        ],
        compiler_params=pltpu.CompilerParams(
            collective_id=0, has_side_effects=True, vmem_limit_bytes=66_000_000
        ),
    )(x, cot, w, kk)
    grad_depth = gd.reshape(2, 25, CH) * keep[None, :, None]
    return (
        dx.reshape(checkpoint.shape),
        jnp.transpose(gp, (1, 0, 2))[None],
        grad_depth[None],
    )


def solution(mesh):
    placed = (
        P("segment", None, "dp", None, None, None),
        P(None, "dp", None, None, None),
        P("segment", None, None, None),
        P("segment", "dp", None, None),
        P("segment"),
    )
    return jax.shard_map(
        body,
        mesh=mesh,
        in_specs=placed,
        out_specs=(
            P("segment", None, "dp", None, None, None),
            P("segment", "dp", None, None),
            P("segment", None, None, None),
        ),
        check_vma=False,
    )
```

```python
import jax
import jax.numpy as jnp
from jax import lax
from jax.experimental import pallas as pl
from jax.experimental.pallas import tpu as pltpu
from jax.sharding import PartitionSpec as P

BF = jnp.bfloat16
F32 = jnp.float32
MESH = pl.DeviceIdType.MESH
PIX = 256
CH = 1024
ROW = 160
PADDED = 20 * ROW
SCALE = 1.0 / 32


def tap_mask(operation):
    tap_ids = jnp.arange(25, dtype=jnp.int32)
    row_off = tap_ids // 5 - 2
    col_off = tap_ids % 5 - 2
    narrow = (jnp.abs(row_off) <= 1) & (jnp.abs(col_off) <= 1)
    dilated = (row_off % 2 == 0) & (col_off % 2 == 0)
    kept_taps = jnp.where(operation == 0, narrow, jnp.where(operation == 1, True, dilated))
    return kept_taps.astype(F32)


def dot_nn(a, b):
    return lax.dot_general(a, b, (((1,), (0,)), ((), ())), preferred_element_type=F32)


def dot_nt(a, b):
    return lax.dot_general(a, b, (((1,), (1,)), ((), ())), preferred_element_type=F32)


def dot_tn(a, b):
    return lax.dot_general(a, b, (((0,), (0,)), ((), ())), preferred_element_type=F32)


def kernel(
    x_hbm, cot_hbm, w_hbm, kk_hbm,
    dx_out, gp_out, gd_out,
    wb, pb, xb, kkb, apad, epad, gpad, bpad, slope, bb, fb, dcb, dyb, dxr,
    r0, ra1, ra2, sa1, sa2, rb1, rb2, sb1, sb2,
    kgf, kgs, kgc, kgt, kgy, kgu, kgx, kgv, kgw,
    ls, ss, rs, turn,
):
    seg = lax.axis_index("segment")
    dp = lax.axis_index("dp")
    z, xl = lax.div(seg, 2), lax.rem(seg, 2)
    xh, y, c = lax.div(dp, 8), lax.rem(lax.div(dp, 2), 4), lax.rem(dp, 2)
    x = xh * 2 + xl
    home = 1 - xl
    mine = 1 - xl

    def at(x_, y_, z_, c_):
        return (z_ * 2 + lax.rem(x_, 2), lax.div(x_, 2) * 8 + y_ * 2 + c_)

    def turn4(v, by):
        return lax.rem(v + by, 4)

    x1, x2, x3 = turn4(x, 1), turn4(x, 2), turn4(x, 3)
    y1, y2, y3 = turn4(y, 1), turn4(y, 2), turn4(y, 3)
    right, far_x, left = at(x1, y, z, c), at(x2, y, z, c), at(x3, y, z, c)
    up, far_y, down = at(x, y1, z, c), at(x, y2, z, c), at(x, y3, z, c)
    sibling = at(x, y, z, 1 - c)
    partner = at(xh * 2 + 1 - xl, y, z, c)
    ahead = at(x, y, lax.rem(z + 7, 8), c)
    behind = at(x, y, lax.rem(z + 1, 8), c)

    def remote(src, dst, k, device):
        return pltpu.make_async_remote_copy(
            src_ref=src, dst_ref=dst, send_sem=ss.at[k], recv_sem=rs.at[k],
            device_id=device, device_id_type=MESH,
        )

    def local(src, dst, k):
        return pltpu.make_async_copy(src, dst, ls.at[k])

    barrier = pltpu.get_barrier_semaphore()
    greeted = (right, far_x, left, up, far_y, down, sibling, ahead, behind)
    for device in greeted:
        pl.semaphore_signal(barrier, inc=1, device_id=device, device_id_type=MESH)

    loads = [
        local(w_hbm, wb.at[home, :, xh, y, c], 0),
        local(x_hbm.at[mine], xb.at[home], 1),
        local(kk_hbm, kkb.at[home], 2),
    ]
    for load in loads:
        load.start()

    @pl.loop(0, 20)
    def _(r):
        nothing = jnp.zeros((ROW, 128), F32)
        for pad in (apad, epad, gpad, bpad):
            for i in range(2):
                pad[i, pl.ds(r * ROW, ROW), :] = nothing

    pl.semaphore_wait(barrier, len(greeted))

    for load in loads:
        load.wait()
    sent = []

    def go(src, dst, k, device):
        copy = remote(src, dst, k, device)
        copy.start()
        sent.append(copy)
        return copy

    def place_x(r):
        return 1 - lax.rem(r, 2), lax.div(r, 2)

    def cell(which, xr, yr, lo=0, n=64):
        s, h = place_x(xr)
        return wb.at[s, which, h, yr, c, pl.ds(lo, n)]

    def xa(r):
        s, h = place_x(r)
        return wb.at[s, 0, h, :, c]

    def ybk(r):
        return wb.at[:, 1, :, r, c]

    def push(ref, k, device):
        return go(ref, ref, k, device)

    a1p = push(cell(0, x, y), 0, up)
    a1m = push(cell(0, x, y), 1, down)
    b1p = push(cell(1, x, y), 2, right)
    b1m = push(cell(1, x, y), 3, left)
    a2r = [push(cell(0, x, y), 73, right)]
    a2l = [push(cell(0, x, y), 77, left)]
    b2u = [push(cell(1, x, y), 81, up)]
    b2d = [push(cell(1, x, y), 85, down)]
    kx = remote(kk_hbm, kkb.at[home], 4, partner)
    xx = remote(x_hbm.at[xl], xb.at[home], 5, partner)

    def to_pixels(pad, i, g, v, row=0):
        for p in range(v.shape[0] // 16):
            start = (p + row + 2) * ROW + 16 + g
            pad[i, pl.ds(start, 16, stride=8), :] = v[p * 16 : p * 16 + 16]

    def spread_activation(i):
        for g in range(8):
            v = jnp.maximum(xb[i, :, g * 128 : g * 128 + 128].astype(F32), 0.0)
            to_pixels(apad, i, g, v)

    def conv(pad, i, which, lo, hi, finish):
        def step(p, _):
            acc = jnp.zeros((16, 8, 128), F32)
            for a in range(5):
                line = pad[i, pl.ds((p + a) * ROW, ROW), :].reshape(20, 8, 128)
                for b in range(5):
                    tap = kkb[i, which, pl.ds((a * 5 + b) * 8, 8), :]
                    acc = acc + line[b : b + 16] * tap[None]
            by_group = jnp.swapaxes(acc, 0, 1)
            here = pl.ds(pl.multiple_of(p * 16, 16), 16)
            for g in range(8):
                finish(here, slice(g * 128, g * 128 + 128), by_group[g])
            return 0

        lax.fori_loop(lo, hi, step, 0)

    def conv_back(pad, i, which, lo, hi, finish):
        taps = []
        for t in range(25):
            tap = kkb[i, which, pl.ds(t * 8, 8), :]
            taps.append(jnp.concatenate([tap, tap], axis=0).astype(BF))

        def step(half, _):
            p = half * 2
            lines = []
            for a in range(6):
                line = pad[i, pl.ds((p + a) * ROW, ROW), :].reshape(20, 8, 128)
                lines.append(jnp.concatenate([line[0:12], line[8:20]], axis=1).astype(BF))
            for r in range(2):
                total = None
                for a in range(5):
                    group = None
                    for b in range(5):
                        term = lines[r + 4 - a][4 - b : 12 - b] * taps[a * 5 + b][None]
                        group = term if group is None else group + term
                    total = group.astype(F32) if total is None else total + group.astype(F32)
                acc = jnp.concatenate([total[:, 0:8], total[:, 8:16]], axis=0)
                by_group = jnp.swapaxes(acc, 0, 1)
                here = pl.ds(pl.multiple_of((p + r) * 16, 16), 16)
                for g in range(8):
                    finish(here, slice(g * 128, g * 128 + 128), by_group[g])
            return 0

        lax.fori_loop(lo // 2, hi // 2, step, 0)

    def rounded_to(ref, i):
        def finish(here, cols, v):
            ref[i, here, cols] = v.astype(BF)

        return finish

    def first_part(i):
        spread_activation(i)
        conv(apad, i, 0, 0, 16, rounded_to(bb, i))

    def second_part(i):
        for n in range(4):
            pre = dot_nn(bb[i], wb[i, 0, :, :, :, :, n * 256 : n * 256 + 256].reshape(CH, 256))
            sg = 1.0 / (1.0 + jnp.exp(-pre))
            slope[i, :, n * 256 : n * 256 + 256] = sg * (1.0 + pre * (1.0 - sg))
            hidden = (pre * sg).astype(BF).astype(F32)
            for g in range(2):
                to_pixels(epad, i, n * 2 + g, hidden[:, g * 128 : g * 128 + 128])

    a1p.wait_recv()
    a1q = push(cell(0, x, y3, 0, 32), 6, up)
    a1m.wait_recv()
    a1n = push(cell(0, x, y1, 32, 32), 7, down)
    b1p.wait_recv()
    b1q = push(cell(1, x3, y, 0, 32), 8, right)
    b1m.wait_recv()
    b1n = push(cell(1, x1, y, 32, 32), 9, left)

    @pl.when(xl == 1)
    def _():
        kx.start()
        xx.start()

    for n, yr in enumerate((y3, y1)):
        a2r.append(push(cell(0, x, yr), 74 + n, right))
        a2l.append(push(cell(0, x, yr), 78 + n, left))
    for n, xr in enumerate((x3, x1)):
        b2u.append(push(cell(1, xr, y), 82 + n, up))
        b2d.append(push(cell(1, xr, y), 86 + n, down))
    a1q.wait_recv()
    a1n.wait_recv()
    a2r.append(push(cell(0, x, y2), 76, right))
    a2l.append(push(cell(0, x, y2), 80, left))
    b1q.wait_recv()
    b1n.wait_recv()
    b2u.append(push(cell(1, x2, y), 84, up))
    b2d.append(push(cell(1, x2, y), 88, down))
    fa = [push(xa(x), 14, sibling)]
    fb_ = [push(ybk(y), 15, sibling)]

    first_part(home)

    a2f, b2f = [], []
    for n, (yr, xr) in enumerate(((y, x), (y3, x3), (y1, x1), (y2, x2))):
        a2r[n].wait_recv()
        a2f.append(push(cell(0, x3, yr), 89 + n, right))
        b2u[n].wait_recv()
        b2f.append(push(cell(1, xr, y3, 0, 32), 93 + n, up))
        b2d[n].wait_recv()
        b2f.append(push(cell(1, xr, y1, 32, 32), 97 + n, down))

    @pl.when(xl == 0)
    def _():
        kx.start()
        xx.start()

    fa.append(push(xa(x3), 20, sibling))
    fb_.append(push(ybk(y3), 22, sibling))
    fb_.append(push(ybk(y1), 23, sibling))
    for copy in a2l:
        copy.wait_recv()
    fa.append(push(xa(x1), 21, sibling))

    kx.wait_recv()
    xx.wait_recv()
    first_part(1 - home)

    for copy in a2f:
        copy.wait_recv()
    fa.append(push(xa(x2), 24, sibling))
    for copy in b2f:
        copy.wait_recv()
    fb_.append(push(ybk(y2), 25, sibling))
    for copy in fa:
        copy.wait_recv()
    second_part(0)

    def third_part(i, _):
        conv(epad, i, 1, 0, 16, rounded_to(fb, i))
        return 0

    @pl.when(z < 7)
    def _():
        second_part(1)
        lax.fori_loop(0, 2, third_part, 0)

    for copy in fb_:
        copy.wait_recv()

    hops = [
        remote(dyb.at[2, pl.ds(k * 64, 64)], dyb.at[0, pl.ds(k * 64, 64)], (26, 54, 55, 56)[k], ahead)
        for k in range(4)
    ]

    @pl.when(z == 7)
    def _():
        load = local(cot_hbm.at[mine], dyb.at[0], 3)
        load.start()
        load.wait()

    def grad_mix(i, lo, n_rows):
        for n in range(4):
            gf = dot_nt(
                dyb[i, pl.ds(lo * 16, n_rows * 16)],
                wb[i, 1, n // 2, pl.ds((n % 2) * 2, 2)].reshape(256, CH),
            )
            for g in range(2):
                to_pixels(gpad, i, n * 2 + g, gf[:, g * 128 : g * 128 + 128], lo)

    def grad_lin(i):
        for n in range(4):
            gl = dot_nt(dcb[i], wb[i, 0, n // 2, pl.ds((n % 2) * 2, 2)].reshape(256, CH))
            for g in range(2):
                to_pixels(bpad, i, n * 2 + g, gl[:, g * 128 : g * 128 + 128])

    def through_slope(i):
        def finish(here, cols, v):
            dcb[i, here, cols] = (v * slope[i, here, cols]).astype(BF)

        return finish

    def onto_input(i):
        def finish(here, cols, v):
            kept = jnp.where(xb[i, here, cols].astype(F32) > 0, v, 0.0)
            dyb[i + 1, here, cols] = (dyb[i, here, cols].astype(F32) + kept).astype(BF)

        return finish

    done = 0
    for k, ready in enumerate((0, 6, 10, 16)):
        @pl.when(z < 7)
        def _():
            hops[k].wait_recv()

        grad_mix(0, k * 4, 4)
        if ready > done:
            conv_back(gpad, 0, 1, done, ready, through_slope(0))
        done = ready
    grad_lin(0)
    conv_back(bpad, 0, 0, 0, 16, onto_input(0))

    backs = [
        remote(dyb.at[1 + xl, pl.ds(k * 64, 64)], dxr.at[pl.ds(k * 64, 64)], (27, 101, 102, 103)[k], partner)
        for k in range(4)
    ]

    @pl.when(xl == 0)
    def _():
        for copy in backs:
            copy.start()

    @pl.when(z == 7)
    def _():
        second_part(1)

    grad_mix(1, 0, 16)
    conv_back(gpad, 1, 1, 0, 16, through_slope(1))
    grad_lin(1)
    for k in range(4):
        conv_back(bpad, 1, 0, k * 4, k * 4 + 4, onto_input(1))

        @pl.when(z > 0)
        def _():
            if k == 0:
                @pl.when((z == 7) & (c == 1))
                def _():
                    pl.semaphore_wait(turn, 1)

            hops[k].start()

        @pl.when(xl == 1)
        def _():
            backs[k].start()

    @pl.when((z == 7) & (c == 0))
    def _():
        for hop in hops:
            hop.wait_send()
        pl.semaphore_signal(turn, inc=1, device_id=sibling, device_id_type=MESH)

    @pl.when(z == 7)
    def _():
        lax.fori_loop(0, 2, third_part, 0)

    def weigh(i, _):
        for n in range(4):
            cols = slice(n * 256, n * 256 + 256)
            first = dot_tn(bb[i, :, cols], dcb[i])
            pb[i, 0, n // 2, pl.ds((n % 2) * 2, 2)] = first.astype(BF).reshape(2, 2, 64, CH)
            second = dot_tn(fb[i, :, cols], dyb[i])
            pb[i, 1, n // 2, pl.ds((n % 2) * 2, 2)] = second.astype(BF).reshape(2, 2, 64, CH)
        return 0

    lax.fori_loop(0, 2, weigh, 0)

    def tap_sums(i, which, vpad, tpad):
        def step(p, totals):
            grad = tpad[i, pl.ds((p + 2) * ROW + 16, 128), :].reshape(16, 8, 128)
            out = []
            for a in range(5):
                line = vpad[i, pl.ds((p + a) * ROW, ROW), :].reshape(20, 8, 128)
                for b in range(5):
                    out.append(totals[a * 5 + b] + jnp.sum(line[b : b + 16] * grad, axis=0))
            return tuple(out)

        totals = lax.fori_loop(0, 16, step, tuple(jnp.zeros((8, 128), F32) for _ in range(25)))
        for t in range(25):
            kgf[i, pl.ds(which * 200 + t * 8, 8), :] = totals[t]

    def gya(r, core, lo=0, n=2):
        return pb.at[pl.ds(lo, n), 0, :, r, core]

    def gxb(r, core, lo=0, n=4):
        s, h = place_x(r)
        return pb.at[s, 1, h, pl.ds(lo, n), core]

    def gxa(r, lo=0, n=64):
        s, h = place_x(r)
        return pb.at[s, 0, h, y, c, pl.ds(lo, n)]

    def gyb(r, lo=0, n=64):
        return pb.at[home, 1, xh, r, c, pl.ds(lo, n)]

    def r0a(r):
        return r0.at[0, :, :, r]

    def r0b(r):
        s, h = place_x(r)
        return r0.at[1, s, h]

    def plus(ref, *others):
        total = ref[...].astype(F32)
        for other in others:
            total = total + other[...].astype(F32)
        return total

    pair_a = {}
    pair_b = {}
    for n, (ry, rx) in enumerate(((y2, x2), (y1, x1), (y3, x3), (y, x))):
        pair_a[n] = go(gya(ry, 1 - c), r0a(ry), 57 + n, sibling)
        pair_b[n] = go(gxb(rx, 1 - c), r0b(rx), 61 + n, sibling)

    def merge_a(n, r):
        pair_a[n].wait_recv()
        ref = gya(r, c)
        ref[...] = plus(ref, r0a(r)).astype(BF)

    def merge_b(n, r):
        pair_b[n].wait_recv()
        ref = gxb(r, c)
        ref[...] = plus(ref, r0b(r)).astype(BF)

    merge_a(0, y2)
    d1p = go(gya(y2, c, 0, 1), ra1.at[0], 31, up)
    d1m = go(gya(y2, c, 1, 1), ra1.at[1], 32, down)
    merge_b(0, x2)
    e1p = go(gxb(x2, c, 0, 2), rb1.at[0], 33, right)
    e1m = go(gxb(x2, c, 2, 2), rb1.at[1], 34, left)
    merge_a(1, y1)
    d2p = [go(gya(y1, c, 1, 1), ra2.at[0, 1:2], 38, up)]
    merge_a(2, y3)
    d2m = [go(gya(y3, c, 0, 1), ra2.at[1, 0:1], 39, down)]
    merge_b(1, x1)
    e2p = [go(gxb(x1, c, 2, 2), rb2.at[0, 2:4], 40, right)]
    merge_b(2, x3)
    e2m = [go(gxb(x3, c, 0, 2), rb2.at[1, 0:2], 41, left)]
    tap_sums(0, 0, apad, bpad)
    tap_sums(0, 1, epad, gpad)

    def pass_on(first, ref, arrived, dst, k, device):
        first.wait_recv()
        ref[...] = plus(ref, arrived).astype(BF)
        return go(ref, dst, k, device)

    d2p.append(pass_on(d1p, gya(y1, c, 0, 1), ra1.at[0], ra2.at[0, 0:1], 65, up))
    d2m.append(pass_on(d1m, gya(y3, c, 1, 1), ra1.at[1], ra2.at[1, 1:2], 66, down))
    e2p.append(pass_on(e1p, gxb(x1, c, 0, 2), rb1.at[0], rb2.at[0, 0:2], 67, right))
    e2m.append(pass_on(e1m, gxb(x3, c, 2, 2), rb1.at[1], rb2.at[1, 2:4], 68, left))
    merge_a(3, y)
    merge_b(3, x)
    tap_sums(1, 0, apad, bpad)
    tap_sums(1, 1, epad, gpad)
    kgs[...] = kgf[1 - c].astype(BF)
    k0 = go(kgs, kgc, 30, sibling)

    k0.wait_recv()
    kgt[...] = (kgf[c] + kgc[...].astype(F32)).astype(BF)
    ky = [go(kgt, kgy.at[j], 35 + j, device) for j, device in enumerate((up, far_y, down))]

    for copy in d2p + d2m:
        copy.wait_recv()
    gya(y, c)[...] = plus(gya(y, c), ra2.at[0], ra2.at[1]).astype(BF)
    d3p = go(gxa(x2, 0, 32), sa1.at[0], 45, right)
    d3m = go(gxa(x2, 32, 32), sa1.at[1], 46, left)
    d4p = [go(gxa(x1, 32, 32), sa2.at[0, 32:64], 50, right)]
    d4m = [go(gxa(x3, 0, 32), sa2.at[1, 0:32], 51, left)]
    for copy in ky:
        copy.wait_recv()
    kgu[...] = plus(kgt, kgy.at[0], kgy.at[1], kgy.at[2]).astype(BF)
    kq = [go(kgu, kgx.at[j], 42 + j, device) for j, device in enumerate((right, far_x, left))]

    for copy in e2p + e2m:
        copy.wait_recv()
    gxb(x, c)[...] = plus(gxb(x, c), rb2.at[0], rb2.at[1]).astype(BF)
    e3p = go(gyb(y2, 0, 32), sb1.at[0], 47, up)
    e3m = go(gyb(y2, 32, 32), sb1.at[1], 48, down)
    e4p = [go(gyb(y1, 32, 32), sb2.at[0, 32:64], 52, up)]
    e4m = [go(gyb(y3, 0, 32), sb2.at[1, 0:32], 53, down)]

    d4p.append(pass_on(d3p, gxa(x1, 0, 32), sa1.at[0], sa2.at[0, 0:32], 69, right))
    d4m.append(pass_on(d3m, gxa(x3, 32, 32), sa1.at[1], sa2.at[1, 32:64], 70, left))
    e4p.append(pass_on(e3p, gyb(y1, 0, 32), sb1.at[0], sb2.at[0, 0:32], 71, up))
    e4m.append(pass_on(e3m, gyb(y3, 32, 32), sb1.at[1], sb2.at[1, 32:64], 72, down))

    for copy in backs:
        copy.wait_recv()
    store0 = local(dyb.at[home + 1], dx_out.at[mine], 4)
    store1 = local(dxr, dx_out.at[1 - mine], 5)
    store0.start()
    store1.start()

    for copy in d4p + d4m:
        copy.wait_recv()
    gp_out[0] = plus(gxa(x), sa2.at[0], sa2.at[1]) * SCALE
    for copy in e4p + e4m:
        copy.wait_recv()
    gp_out[1] = plus(gyb(y), sb2.at[0], sb2.at[1]) * SCALE

    for copy in kq:
        copy.wait_recv()
    kgv[...] = plus(kgu, kgx.at[0], kgx.at[1], kgx.at[2]).astype(BF)
    k3 = go(kgv, kgw, 49, sibling)
    k3.wait_recv()
    own = (c == home).astype(F32)
    gd_out[...] = (kgv[...].astype(F32) * own + kgw[...].astype(F32) * (1.0 - own)) * SCALE

    store0.wait()
    store1.wait()
    for copy in sent + backs + [kx, xx]:
        copy.wait_send()

    @pl.when((z > 0) & ((z < 7) | (c == 1)))
    def _():
        for hop in hops:
            hop.wait_send()


def body(checkpoint, cotangent, depthwise, pointwise, genotype):
    x = checkpoint.reshape(2, PIX, CH)
    cot = cotangent.reshape(2, PIX, CH)
    keep = tap_mask(genotype[0])
    kk = (depthwise[0] * keep[None, :, None]).reshape(2, 200, 128)
    w = jnp.transpose(pointwise[0], (1, 0, 2))
    anywhere = pl.BlockSpec(memory_space=pl.ANY)
    here = pl.BlockSpec(memory_space=pltpu.VMEM)
    pad = pltpu.VMEM((2, PADDED, 128), F32)
    taps = pltpu.VMEM((400, 128), BF)
    image2 = pltpu.VMEM((2, PIX, CH), BF)
    dx, gp, gd = pl.pallas_call(
        kernel,
        out_shape=(
            jax.ShapeDtypeStruct((2, PIX, CH), BF),
            jax.ShapeDtypeStruct((2, 64, CH), F32),
            jax.ShapeDtypeStruct((400, 128), F32),
        ),
        in_specs=[anywhere] * 4,
        out_specs=(anywhere, here, here),
        scratch_shapes=[
            pltpu.VMEM((2, 2, 2, 4, 2, 64, CH), BF),
            pltpu.VMEM((2, 2, 2, 4, 2, 64, CH), BF),
            image2,
            pltpu.VMEM((2, 2, 200, 128), F32),
            pad, pad, pad, pad,
            pltpu.VMEM((2, PIX, CH), F32),
            image2, image2, image2,
            pltpu.VMEM((3, PIX, CH), BF),
            pltpu.VMEM((PIX, CH), BF),
            pltpu.VMEM((2, 2, 2, 4, 64, CH), BF),
            pltpu.VMEM((2, 1, 2, 64, CH), BF),
            pltpu.VMEM((2, 2, 2, 64, CH), BF),
            pltpu.VMEM((2, 32, CH), BF),
            pltpu.VMEM((2, 64, CH), BF),
            pltpu.VMEM((2, 2, 64, CH), BF),
            pltpu.VMEM((2, 4, 64, CH), BF),
            pltpu.VMEM((2, 32, CH), BF),
            pltpu.VMEM((2, 64, CH), BF),
            pltpu.VMEM((2, 400, 128), F32),
            taps, taps, taps,
            pltpu.VMEM((3, 400, 128), BF),
            taps,
            pltpu.VMEM((3, 400, 128), BF),
            taps, taps,
            pltpu.SemaphoreType.DMA((6,)),
            pltpu.SemaphoreType.DMA((104,)),
            pltpu.SemaphoreType.DMA((104,)),
            pltpu.SemaphoreType.REGULAR,
        ],
        compiler_params=pltpu.CompilerParams(
            collective_id=0, has_side_effects=True, vmem_limit_bytes=66_000_000
        ),
    )(x, cot, w, kk)
    grad_depth = gd.reshape(2, 25, CH) * keep[None, :, None]
    return (
        dx.reshape(checkpoint.shape),
        jnp.transpose(gp, (1, 0, 2))[None],
        grad_depth[None],
    )


def solution(mesh):
    placed = (
        P("segment", None, "dp", None, None, None),
        P(None, "dp", None, None, None),
        P("segment", None, None, None),
        P("segment", "dp", None, None),
        P("segment"),
    )
    return jax.shard_map(
        body,
        mesh=mesh,
        in_specs=placed,
        out_specs=(
            P("segment", None, "dp", None, None, None),
            P("segment", "dp", None, None),
            P("segment", None, None, None),
        ),
        check_vma=False,
    )
```

```python
import jax
import jax.numpy as jnp
from jax import lax
from jax.experimental import pallas as pl
from jax.experimental.pallas import tpu as pltpu
from jax.sharding import PartitionSpec as P

BF = jnp.bfloat16
F32 = jnp.float32
MESH = pl.DeviceIdType.MESH
PIX = 256
CH = 1024
ROW = 160
PADDED = 20 * ROW
SCALE = 1.0 / 32


def tap_mask(operation):
    tap_ids = jnp.arange(25, dtype=jnp.int32)
    row_off = tap_ids // 5 - 2
    col_off = tap_ids % 5 - 2
    narrow = (jnp.abs(row_off) <= 1) & (jnp.abs(col_off) <= 1)
    dilated = (row_off % 2 == 0) & (col_off % 2 == 0)
    kept_taps = jnp.where(operation == 0, narrow, jnp.where(operation == 1, True, dilated))
    return kept_taps.astype(F32)


def dot_nn(a, b):
    return lax.dot_general(a, b, (((1,), (0,)), ((), ())), preferred_element_type=F32)


def dot_nt(a, b):
    return lax.dot_general(a, b, (((1,), (1,)), ((), ())), preferred_element_type=F32)


def dot_tn(a, b):
    return lax.dot_general(a, b, (((0,), (0,)), ((), ())), preferred_element_type=F32)


def kernel(
    x_hbm, cot_hbm, w_hbm, kk_hbm,
    dx_out, gp_out, gd_out,
    wb, pb, xb, kkb, apad, epad, gpad, bpad, slope, bb, fb, dcb, dyb, dxr,
    r0, ra1, ra2, sa1, sa2, rb1, rb2, sb1, sb2,
    kgf, kgs, kgc, kgt, kgy, kgu, kgx, kgv, kgw,
    ls, ss, rs, turn,
):
    seg = lax.axis_index("segment")
    dp = lax.axis_index("dp")
    z, xl = lax.div(seg, 2), lax.rem(seg, 2)
    xh, y, c = lax.div(dp, 8), lax.rem(lax.div(dp, 2), 4), lax.rem(dp, 2)
    x = xh * 2 + xl
    home = 1 - xl
    mine = 1 - xl

    def at(x_, y_, z_, c_):
        return (z_ * 2 + lax.rem(x_, 2), lax.div(x_, 2) * 8 + y_ * 2 + c_)

    def turn4(v, by):
        return lax.rem(v + by, 4)

    x1, x2, x3 = turn4(x, 1), turn4(x, 2), turn4(x, 3)
    y1, y2, y3 = turn4(y, 1), turn4(y, 2), turn4(y, 3)
    right, far_x, left = at(x1, y, z, c), at(x2, y, z, c), at(x3, y, z, c)
    up, far_y, down = at(x, y1, z, c), at(x, y2, z, c), at(x, y3, z, c)
    sibling = at(x, y, z, 1 - c)
    partner = at(xh * 2 + 1 - xl, y, z, c)
    ahead = at(x, y, lax.rem(z + 7, 8), c)
    behind = at(x, y, lax.rem(z + 1, 8), c)

    def remote(src, dst, k, device):
        return pltpu.make_async_remote_copy(
            src_ref=src, dst_ref=dst, send_sem=ss.at[k], recv_sem=rs.at[k],
            device_id=device, device_id_type=MESH,
        )

    def local(src, dst, k):
        return pltpu.make_async_copy(src, dst, ls.at[k])

    barrier = pltpu.get_barrier_semaphore()
    greeted = (right, far_x, left, up, far_y, down, sibling, ahead, behind)
    for device in greeted:
        pl.semaphore_signal(barrier, inc=1, device_id=device, device_id_type=MESH)

    loads = [
        local(w_hbm, wb.at[home, :, xh, y, c], 0),
        local(x_hbm.at[mine], xb.at[home], 1),
        local(kk_hbm, kkb.at[home], 2),
    ]
    for load in loads:
        load.start()

    @pl.loop(0, 20)
    def _(r):
        nothing = jnp.zeros((ROW, 128), F32)
        for pad in (apad, epad, gpad, bpad):
            for i in range(2):
                pad[i, pl.ds(r * ROW, ROW), :] = nothing

    pl.semaphore_wait(barrier, len(greeted))

    for load in loads:
        load.wait()
    sent = []

    def go(src, dst, k, device):
        copy = remote(src, dst, k, device)
        copy.start()
        sent.append(copy)
        return copy

    def place_x(r):
        return 1 - lax.rem(r, 2), lax.div(r, 2)

    def cell(which, xr, yr, lo=0, n=64):
        s, h = place_x(xr)
        return wb.at[s, which, h, yr, c, pl.ds(lo, n)]

    def xa(r):
        s, h = place_x(r)
        return wb.at[s, 0, h, :, c]

    def ybk(r):
        return wb.at[:, 1, :, r, c]

    def push(ref, k, device):
        return go(ref, ref, k, device)

    a1p = push(cell(0, x, y), 0, up)
    a1m = push(cell(0, x, y), 1, down)
    b1p = push(cell(1, x, y), 2, right)
    b1m = push(cell(1, x, y), 3, left)
    a2r = [push(cell(0, x, y), 73, right)]
    a2l = [push(cell(0, x, y), 77, left)]
    b2u = [push(cell(1, x, y), 81, up)]
    b2d = [push(cell(1, x, y), 85, down)]
    kx = remote(kk_hbm, kkb.at[home], 4, partner)
    xx = remote(x_hbm.at[xl], xb.at[home], 5, partner)

    def to_pixels(pad, i, g, v, row=0):
        for p in range(v.shape[0] // 16):
            start = (p + row + 2) * ROW + 16 + g
            pad[i, pl.ds(start, 16, stride=8), :] = v[p * 16 : p * 16 + 16]

    def spread_activation(i):
        for g in range(8):
            v = jnp.maximum(xb[i, :, g * 128 : g * 128 + 128].astype(F32), 0.0)
            to_pixels(apad, i, g, v)

    def conv(pad, i, which, lo, hi, finish):
        def step(p, _):
            acc = jnp.zeros((16, 8, 128), F32)
            for a in range(5):
                line = pad[i, pl.ds((p + a) * ROW, ROW), :].reshape(20, 8, 128)
                for b in range(5):
                    tap = kkb[i, which, pl.ds((a * 5 + b) * 8, 8), :]
                    acc = acc + line[b : b + 16] * tap[None]
            by_group = jnp.swapaxes(acc, 0, 1)
            here = pl.ds(pl.multiple_of(p * 16, 16), 16)
            for g in range(8):
                finish(here, slice(g * 128, g * 128 + 128), by_group[g])
            return 0

        lax.fori_loop(lo, hi, step, 0)

    def conv_back(pad, i, which, lo, hi, finish):
        taps = []
        for t in range(25):
            tap = kkb[i, which, pl.ds(t * 8, 8), :]
            taps.append(jnp.concatenate([tap, tap], axis=0).astype(BF))

        def step(half, _):
            p = half * 2
            lines = []
            for a in range(6):
                line = pad[i, pl.ds((p + a) * ROW, ROW), :].reshape(20, 8, 128)
                lines.append(jnp.concatenate([line[0:12], line[8:20]], axis=1).astype(BF))
            for r in range(2):
                total = None
                for a in range(5):
                    group = None
                    for b in range(5):
                        term = lines[r + 4 - a][4 - b : 12 - b] * taps[a * 5 + b][None]
                        group = term if group is None else group + term
                    total = group.astype(F32) if total is None else total + group.astype(F32)
                acc = jnp.concatenate([total[:, 0:8], total[:, 8:16]], axis=0)
                by_group = jnp.swapaxes(acc, 0, 1)
                here = pl.ds(pl.multiple_of((p + r) * 16, 16), 16)
                for g in range(8):
                    finish(here, slice(g * 128, g * 128 + 128), by_group[g])
            return 0

        lax.fori_loop(lo // 2, hi // 2, step, 0)

    def rounded_to(ref, i):
        def finish(here, cols, v):
            ref[i, here, cols] = v.astype(BF)

        return finish

    def first_part(i):
        spread_activation(i)
        conv(apad, i, 0, 0, 16, rounded_to(bb, i))

    def second_part(i):
        for n in range(4):
            pre = dot_nn(bb[i], wb[i, 0, :, :, :, :, n * 256 : n * 256 + 256].reshape(CH, 256))
            sg = 1.0 / (1.0 + jnp.exp(-pre))
            slope[i, :, n * 256 : n * 256 + 256] = sg * (1.0 + pre * (1.0 - sg))
            hidden = (pre * sg).astype(BF).astype(F32)
            for g in range(2):
                to_pixels(epad, i, n * 2 + g, hidden[:, g * 128 : g * 128 + 128])

    a1p.wait_recv()
    a1q = push(cell(0, x, y3, 0, 32), 6, up)
    a1m.wait_recv()
    a1n = push(cell(0, x, y1, 32, 32), 7, down)
    b1p.wait_recv()
    b1q = push(cell(1, x3, y, 0, 32), 8, right)
    b1m.wait_recv()
    b1n = push(cell(1, x1, y, 32, 32), 9, left)

    for n, yr in enumerate((y3, y1)):
        a2r.append(push(cell(0, x, yr), 74 + n, right))
        a2l.append(push(cell(0, x, yr), 78 + n, left))
    for n, xr in enumerate((x3, x1)):
        b2u.append(push(cell(1, xr, y), 82 + n, up))
        b2d.append(push(cell(1, xr, y), 86 + n, down))
    a1q.wait_recv()
    a1n.wait_recv()
    a2r.append(push(cell(0, x, y2), 76, right))
    a2l.append(push(cell(0, x, y2), 80, left))
    b1q.wait_recv()
    b1n.wait_recv()
    b2u.append(push(cell(1, x2, y), 84, up))
    b2d.append(push(cell(1, x2, y), 88, down))
    kx.start()
    xx.start()
    fa = [push(xa(x), 14, sibling)]
    fb_ = [push(ybk(y), 15, sibling)]

    first_part(home)

    passed = turn4(x, 1 + 2 * xl)
    onward = at(turn4(x, 3 - 2 * xl), y, z, c)
    a2f, b2f = [], []
    for n, (yr, xr) in enumerate(((y, x), (y3, x3), (y1, x1), (y2, x2))):
        a2r[n].wait_recv()
        a2l[n].wait_recv()
        a2f.append(push(cell(0, passed, yr), 89 + n, onward))
        b2u[n].wait_recv()
        b2f.append(push(cell(1, xr, y3, 0, 32), 93 + n, up))
        b2d[n].wait_recv()
        b2f.append(push(cell(1, xr, y1, 32, 32), 97 + n, down))

    fa.append(push(xa(x3), 20, sibling))
    fb_.append(push(ybk(y3), 22, sibling))
    fb_.append(push(ybk(y1), 23, sibling))
    fa.append(push(xa(x1), 21, sibling))
    for copy in a2f:
        copy.wait_recv()
    fa.append(push(xa(x2), 24, sibling))
    for copy in b2f:
        copy.wait_recv()
    fb_.append(push(ybk(y2), 25, sibling))

    def other_input():
        kx.wait_recv()
        xx.wait_recv()
        first_part(1 - home)

    @pl.when((z < 7) | (xl == 0))
    def _():
        other_input()

    for copy in fa:
        copy.wait_recv()
    second_part(0)

    def third_part(i, _):
        conv(epad, i, 1, 0, 16, rounded_to(fb, i))
        return 0

    @pl.when(z < 7)
    def _():
        second_part(1)
        lax.fori_loop(0, 2, third_part, 0)

    for copy in fb_:
        copy.wait_recv()

    hops = [
        remote(dyb.at[2, pl.ds(k * 64, 64)], dyb.at[0, pl.ds(k * 64, 64)], (26, 54, 55, 56)[k], ahead)
        for k in range(4)
    ]

    @pl.when(z == 7)
    def _():
        load = local(cot_hbm.at[mine], dyb.at[0], 3)
        load.start()
        load.wait()

    def grad_mix(i, lo, n_rows):
        for n in range(4):
            gf = dot_nt(
                dyb[i, pl.ds(lo * 16, n_rows * 16)],
                wb[i, 1, n // 2, pl.ds((n % 2) * 2, 2)].reshape(256, CH),
            )
            for g in range(2):
                to_pixels(gpad, i, n * 2 + g, gf[:, g * 128 : g * 128 + 128], lo)

    def grad_lin(i):
        for n in range(4):
            gl = dot_nt(dcb[i], wb[i, 0, n // 2, pl.ds((n % 2) * 2, 2)].reshape(256, CH))
            for g in range(2):
                to_pixels(bpad, i, n * 2 + g, gl[:, g * 128 : g * 128 + 128])

    def through_slope(i):
        def finish(here, cols, v):
            dcb[i, here, cols] = (v * slope[i, here, cols]).astype(BF)

        return finish

    def onto_input(i):
        def finish(here, cols, v):
            kept = jnp.where(xb[i, here, cols].astype(F32) > 0, v, 0.0)
            dyb[i + 1, here, cols] = (dyb[i, here, cols].astype(F32) + kept).astype(BF)

        return finish

    done = 0
    for k, ready in enumerate((0, 6, 10, 16)):
        @pl.when(z < 7)
        def _():
            hops[k].wait_recv()

        grad_mix(0, k * 4, 4)
        if ready > done:
            conv_back(gpad, 0, 1, done, ready, through_slope(0))
        done = ready
    grad_lin(0)
    conv_back(bpad, 0, 0, 0, 16, onto_input(0))

    backs = [
        remote(dyb.at[1 + xl, pl.ds(k * 64, 64)], dxr.at[pl.ds(k * 64, 64)], (27, 101, 102, 103)[k], partner)
        for k in range(4)
    ]

    @pl.when(xl == 0)
    def _():
        for copy in backs:
            copy.start()

    @pl.when((z == 7) & (xl == 1))
    def _():
        other_input()

    @pl.when(z == 7)
    def _():
        second_part(1)

    grad_mix(1, 0, 16)
    conv_back(gpad, 1, 1, 0, 16, through_slope(1))
    grad_lin(1)
    for k in range(4):
        conv_back(bpad, 1, 0, k * 4, k * 4 + 4, onto_input(1))

        @pl.when(z > 0)
        def _():
            if k == 0:
                @pl.when((z == 7) & (c == 1))
                def _():
                    pl.semaphore_wait(turn, 1)

            hops[k].start()

        @pl.when(xl == 1)
        def _():
            backs[k].start()

    @pl.when((z == 7) & (c == 0))
    def _():
        for hop in hops:
            hop.wait_send()
        pl.semaphore_signal(turn, inc=1, device_id=sibling, device_id_type=MESH)

    @pl.when(z == 7)
    def _():
        lax.fori_loop(0, 2, third_part, 0)

    def weigh(i, _):
        for n in range(4):
            cols = slice(n * 256, n * 256 + 256)
            first = dot_tn(bb[i, :, cols], dcb[i])
            pb[i, 0, n // 2, pl.ds((n % 2) * 2, 2)] = first.astype(BF).reshape(2, 2, 64, CH)
            second = dot_tn(fb[i, :, cols], dyb[i])
            pb[i, 1, n // 2, pl.ds((n % 2) * 2, 2)] = second.astype(BF).reshape(2, 2, 64, CH)
        return 0

    lax.fori_loop(0, 2, weigh, 0)

    def tap_sums(i, which, vpad, tpad):
        def step(p, totals):
            grad = tpad[i, pl.ds((p + 2) * ROW + 16, 128), :].reshape(16, 8, 128)
            out = []
            for a in range(5):
                line = vpad[i, pl.ds((p + a) * ROW, ROW), :].reshape(20, 8, 128)
                for b in range(5):
                    out.append(totals[a * 5 + b] + jnp.sum(line[b : b + 16] * grad, axis=0))
            return tuple(out)

        totals = lax.fori_loop(0, 16, step, tuple(jnp.zeros((8, 128), F32) for _ in range(25)))
        for t in range(25):
            kgf[i, pl.ds(which * 200 + t * 8, 8), :] = totals[t]

    def gya(r, core, lo=0, n=2):
        return pb.at[pl.ds(lo, n), 0, :, r, core]

    def gxb(r, core, lo=0, n=4):
        s, h = place_x(r)
        return pb.at[s, 1, h, pl.ds(lo, n), core]

    def gxa(r, lo=0, n=64):
        s, h = place_x(r)
        return pb.at[s, 0, h, y, c, pl.ds(lo, n)]

    def gyb(r, lo=0, n=64):
        return pb.at[home, 1, xh, r, c, pl.ds(lo, n)]

    def r0a(r):
        return r0.at[0, :, :, r]

    def r0b(r):
        s, h = place_x(r)
        return r0.at[1, s, h]

    def plus(ref, *others):
        total = ref[...].astype(F32)
        for other in others:
            total = total + other[...].astype(F32)
        return total

    pair_a = {}
    pair_b = {}
    for n, (ry, rx) in enumerate(((y2, x2), (y1, x1), (y3, x3), (y, x))):
        pair_a[n] = go(gya(ry, 1 - c), r0a(ry), 57 + n, sibling)
        pair_b[n] = go(gxb(rx, 1 - c), r0b(rx), 61 + n, sibling)

    def merge_a(n, r):
        pair_a[n].wait_recv()
        ref = gya(r, c)
        ref[...] = plus(ref, r0a(r)).astype(BF)

    def merge_b(n, r):
        pair_b[n].wait_recv()
        ref = gxb(r, c)
        ref[...] = plus(ref, r0b(r)).astype(BF)

    merge_a(0, y2)
    d1p = go(gya(y2, c, 0, 1), ra1.at[0], 31, up)
    d1m = go(gya(y2, c, 1, 1), ra1.at[1], 32, down)
    merge_b(0, x2)
    e1p = go(gxb(x2, c, 0, 2), rb1.at[0], 33, right)
    e1m = go(gxb(x2, c, 2, 2), rb1.at[1], 34, left)
    merge_a(1, y1)
    d2p = [go(gya(y1, c, 1, 1), ra2.at[0, 1:2], 38, up)]
    merge_a(2, y3)
    d2m = [go(gya(y3, c, 0, 1), ra2.at[1, 0:1], 39, down)]
    merge_b(1, x1)
    e2p = [go(gxb(x1, c, 2, 2), rb2.at[0, 2:4], 40, right)]
    merge_b(2, x3)
    e2m = [go(gxb(x3, c, 0, 2), rb2.at[1, 0:2], 41, left)]
    tap_sums(0, 0, apad, bpad)
    tap_sums(0, 1, epad, gpad)

    def pass_on(first, ref, arrived, dst, k, device):
        first.wait_recv()
        ref[...] = plus(ref, arrived).astype(BF)
        return go(ref, dst, k, device)

    d2p.append(pass_on(d1p, gya(y1, c, 0, 1), ra1.at[0], ra2.at[0, 0:1], 65, up))
    d2m.append(pass_on(d1m, gya(y3, c, 1, 1), ra1.at[1], ra2.at[1, 1:2], 66, down))
    e2p.append(pass_on(e1p, gxb(x1, c, 0, 2), rb1.at[0], rb2.at[0, 0:2], 67, right))
    e2m.append(pass_on(e1m, gxb(x3, c, 2, 2), rb1.at[1], rb2.at[1, 2:4], 68, left))
    merge_a(3, y)
    merge_b(3, x)
    tap_sums(1, 0, apad, bpad)
    tap_sums(1, 1, epad, gpad)
    kgs[...] = kgf[1 - c].astype(BF)
    k0 = go(kgs, kgc, 30, sibling)

    k0.wait_recv()
    kgt[...] = (kgf[c] + kgc[...].astype(F32)).astype(BF)
    ky = [go(kgt, kgy.at[j], 35 + j, device) for j, device in enumerate((up, far_y, down))]

    for copy in d2p + d2m:
        copy.wait_recv()
    gya(y, c)[...] = plus(gya(y, c), ra2.at[0], ra2.at[1]).astype(BF)
    d3p = go(gxa(x2, 0, 32), sa1.at[0], 45, right)
    d3m = go(gxa(x2, 32, 32), sa1.at[1], 46, left)
    d4p = [go(gxa(x1, 32, 32), sa2.at[0, 32:64], 50, right)]
    d4m = [go(gxa(x3, 0, 32), sa2.at[1, 0:32], 51, left)]
    for copy in ky:
        copy.wait_recv()
    kgu[...] = plus(kgt, kgy.at[0], kgy.at[1], kgy.at[2]).astype(BF)
    kq = [go(kgu, kgx.at[j], 42 + j, device) for j, device in enumerate((right, far_x, left))]

    for copy in e2p + e2m:
        copy.wait_recv()
    gxb(x, c)[...] = plus(gxb(x, c), rb2.at[0], rb2.at[1]).astype(BF)
    e3p = go(gyb(y2, 0, 32), sb1.at[0], 47, up)
    e3m = go(gyb(y2, 32, 32), sb1.at[1], 48, down)
    e4p = [go(gyb(y1, 32, 32), sb2.at[0, 32:64], 52, up)]
    e4m = [go(gyb(y3, 0, 32), sb2.at[1, 0:32], 53, down)]

    d4p.append(pass_on(d3p, gxa(x1, 0, 32), sa1.at[0], sa2.at[0, 0:32], 69, right))
    d4m.append(pass_on(d3m, gxa(x3, 32, 32), sa1.at[1], sa2.at[1, 32:64], 70, left))
    e4p.append(pass_on(e3p, gyb(y1, 0, 32), sb1.at[0], sb2.at[0, 0:32], 71, up))
    e4m.append(pass_on(e3m, gyb(y3, 32, 32), sb1.at[1], sb2.at[1, 32:64], 72, down))

    for copy in backs:
        copy.wait_recv()
    store0 = local(dyb.at[home + 1], dx_out.at[mine], 4)
    store1 = local(dxr, dx_out.at[1 - mine], 5)
    store0.start()
    store1.start()

    for copy in d4p + d4m:
        copy.wait_recv()
    gp_out[0] = plus(gxa(x), sa2.at[0], sa2.at[1]) * SCALE
    for copy in e4p + e4m:
        copy.wait_recv()
    gp_out[1] = plus(gyb(y), sb2.at[0], sb2.at[1]) * SCALE

    for copy in kq:
        copy.wait_recv()
    kgv[...] = plus(kgu, kgx.at[0], kgx.at[1], kgx.at[2]).astype(BF)
    k3 = go(kgv, kgw, 49, sibling)
    k3.wait_recv()
    own = (c == home).astype(F32)
    gd_out[...] = (kgv[...].astype(F32) * own + kgw[...].astype(F32) * (1.0 - own)) * SCALE

    store0.wait()
    store1.wait()
    for copy in sent + backs + [kx, xx]:
        copy.wait_send()

    @pl.when((z > 0) & ((z < 7) | (c == 1)))
    def _():
        for hop in hops:
            hop.wait_send()


def body(checkpoint, cotangent, depthwise, pointwise, genotype):
    x = checkpoint.reshape(2, PIX, CH)
    cot = cotangent.reshape(2, PIX, CH)
    keep = tap_mask(genotype[0])
    kk = (depthwise[0] * keep[None, :, None]).reshape(2, 200, 128)
    w = jnp.transpose(pointwise[0], (1, 0, 2))
    anywhere = pl.BlockSpec(memory_space=pl.ANY)
    here = pl.BlockSpec(memory_space=pltpu.VMEM)
    pad = pltpu.VMEM((2, PADDED, 128), F32)
    taps = pltpu.VMEM((400, 128), BF)
    image2 = pltpu.VMEM((2, PIX, CH), BF)
    dx, gp, gd = pl.pallas_call(
        kernel,
        out_shape=(
            jax.ShapeDtypeStruct((2, PIX, CH), BF),
            jax.ShapeDtypeStruct((2, 64, CH), F32),
            jax.ShapeDtypeStruct((400, 128), F32),
        ),
        in_specs=[anywhere] * 4,
        out_specs=(anywhere, here, here),
        scratch_shapes=[
            pltpu.VMEM((2, 2, 2, 4, 2, 64, CH), BF),
            pltpu.VMEM((2, 2, 2, 4, 2, 64, CH), BF),
            image2,
            pltpu.VMEM((2, 2, 200, 128), F32),
            pad, pad, pad, pad,
            pltpu.VMEM((2, PIX, CH), F32),
            image2, image2, image2,
            pltpu.VMEM((3, PIX, CH), BF),
            pltpu.VMEM((PIX, CH), BF),
            pltpu.VMEM((2, 2, 2, 4, 64, CH), BF),
            pltpu.VMEM((2, 1, 2, 64, CH), BF),
            pltpu.VMEM((2, 2, 2, 64, CH), BF),
            pltpu.VMEM((2, 32, CH), BF),
            pltpu.VMEM((2, 64, CH), BF),
            pltpu.VMEM((2, 2, 64, CH), BF),
            pltpu.VMEM((2, 4, 64, CH), BF),
            pltpu.VMEM((2, 32, CH), BF),
            pltpu.VMEM((2, 64, CH), BF),
            pltpu.VMEM((2, 400, 128), F32),
            taps, taps, taps,
            pltpu.VMEM((3, 400, 128), BF),
            taps,
            pltpu.VMEM((3, 400, 128), BF),
            taps, taps,
            pltpu.SemaphoreType.DMA((6,)),
            pltpu.SemaphoreType.DMA((104,)),
            pltpu.SemaphoreType.DMA((104,)),
            pltpu.SemaphoreType.REGULAR,
        ],
        compiler_params=pltpu.CompilerParams(
            collective_id=0, has_side_effects=True, vmem_limit_bytes=66_000_000
        ),
    )(x, cot, w, kk)
    grad_depth = gd.reshape(2, 25, CH) * keep[None, :, None]
    return (
        dx.reshape(checkpoint.shape),
        jnp.transpose(gp, (1, 0, 2))[None],
        grad_depth[None],
    )


def solution(mesh):
    placed = (
        P("segment", None, "dp", None, None, None),
        P(None, "dp", None, None, None),
        P("segment", None, None, None),
        P("segment", "dp", None, None),
        P("segment"),
    )
    return jax.shard_map(
        body,
        mesh=mesh,
        in_specs=placed,
        out_specs=(
            P("segment", None, "dp", None, None, None),
            P("segment", "dp", None, None),
            P("segment", None, None, None),
        ),
        check_vma=False,
    )
```

```python
import jax
import jax.numpy as jnp
from jax import lax
from jax.experimental import pallas as pl
from jax.experimental.pallas import tpu as pltpu
from jax.sharding import PartitionSpec as P

BF = jnp.bfloat16
F32 = jnp.float32
MESH = pl.DeviceIdType.MESH
PIX = 256
CH = 1024
ROW = 160
PADDED = 20 * ROW
SCALE = 1.0 / 32


def tap_mask(operation):
    tap_ids = jnp.arange(25, dtype=jnp.int32)
    row_off = tap_ids // 5 - 2
    col_off = tap_ids % 5 - 2
    narrow = (jnp.abs(row_off) <= 1) & (jnp.abs(col_off) <= 1)
    dilated = (row_off % 2 == 0) & (col_off % 2 == 0)
    kept_taps = jnp.where(operation == 0, narrow, jnp.where(operation == 1, True, dilated))
    return kept_taps.astype(F32)


def dot_nn(a, b):
    return lax.dot_general(a, b, (((1,), (0,)), ((), ())), preferred_element_type=F32)


def dot_nt(a, b):
    return lax.dot_general(a, b, (((1,), (1,)), ((), ())), preferred_element_type=F32)


def dot_tn(a, b):
    return lax.dot_general(a, b, (((0,), (0,)), ((), ())), preferred_element_type=F32)


def kernel(
    x_hbm, cot_hbm, w_hbm, kk_hbm,
    dx_out, gp_out, gd_out,
    wb, pb, xb, kkb, apad, epad, gpad, bpad, slope, bb, fb, dcb, dyb, dxr,
    r0, ra1, ra2, sa1, sa2, rb1, rb2, sb1, sb2,
    kgf, kgs, kgc, kgt, kgy, kgu, kgx, kgv, kgw,
    ls, ss, rs, turn,
):
    seg = lax.axis_index("segment")
    dp = lax.axis_index("dp")
    z, xl = lax.div(seg, 2), lax.rem(seg, 2)
    xh, y, c = lax.div(dp, 8), lax.rem(lax.div(dp, 2), 4), lax.rem(dp, 2)
    x = xh * 2 + xl
    home = 1 - xl
    mine = 1 - xl

    def at(x_, y_, z_, c_):
        return (z_ * 2 + lax.rem(x_, 2), lax.div(x_, 2) * 8 + y_ * 2 + c_)

    def turn4(v, by):
        return lax.rem(v + by, 4)

    x1, x2, x3 = turn4(x, 1), turn4(x, 2), turn4(x, 3)
    y1, y2, y3 = turn4(y, 1), turn4(y, 2), turn4(y, 3)
    right, far_x, left = at(x1, y, z, c), at(x2, y, z, c), at(x3, y, z, c)
    up, far_y, down = at(x, y1, z, c), at(x, y2, z, c), at(x, y3, z, c)
    sibling = at(x, y, z, 1 - c)
    partner = at(xh * 2 + 1 - xl, y, z, c)
    ahead = at(x, y, lax.rem(z + 7, 8), c)
    behind = at(x, y, lax.rem(z + 1, 8), c)

    def remote(src, dst, k, device):
        return pltpu.make_async_remote_copy(
            src_ref=src, dst_ref=dst, send_sem=ss.at[k], recv_sem=rs.at[k],
            device_id=device, device_id_type=MESH,
        )

    def local(src, dst, k):
        return pltpu.make_async_copy(src, dst, ls.at[k])

    barrier = pltpu.get_barrier_semaphore()
    greeted = (right, far_x, left, up, far_y, down, sibling, ahead, behind)
    for device in greeted:
        pl.semaphore_signal(barrier, inc=1, device_id=device, device_id_type=MESH)

    loads = [
        local(w_hbm, wb.at[home, :, xh, y, c], 0),
        local(x_hbm.at[mine], xb.at[home], 1),
        local(kk_hbm, kkb.at[home], 2),
    ]
    for load in loads:
        load.start()

    @pl.loop(0, 20)
    def _(r):
        nothing = jnp.zeros((ROW, 128), F32)
        for pad in (apad, epad, gpad, bpad):
            for i in range(2):
                pad[i, pl.ds(r * ROW, ROW), :] = nothing

    pl.semaphore_wait(barrier, len(greeted))

    for load in loads:
        load.wait()
    sent = []

    def go(src, dst, k, device):
        copy = remote(src, dst, k, device)
        copy.start()
        sent.append(copy)
        return copy

    def place_x(r):
        return 1 - lax.rem(r, 2), lax.div(r, 2)

    def cell(which, xr, yr, lo=0, n=64):
        s, h = place_x(xr)
        return wb.at[s, which, h, yr, c, pl.ds(lo, n)]

    def xa(r):
        s, h = place_x(r)
        return wb.at[s, 0, h, :, c]

    def ybk(r):
        return wb.at[:, 1, :, r, c]

    def push(ref, k, device):
        return go(ref, ref, k, device)

    a1p = push(cell(0, x, y), 0, up)
    a1m = push(cell(0, x, y), 1, down)
    b1p = push(cell(1, x, y), 2, right)
    b1m = push(cell(1, x, y), 3, left)
    a2r = [push(cell(0, x, y), 73, right)]
    a2l = [push(cell(0, x, y), 77, left)]
    b2u = [push(cell(1, x, y), 81, up)]
    b2d = [push(cell(1, x, y), 85, down)]
    kx = remote(kk_hbm, kkb.at[home], 4, partner)
    xx = remote(x_hbm.at[xl], xb.at[home], 5, partner)

    def to_pixels(pad, i, g, v, row=0):
        for p in range(v.shape[0] // 16):
            start = (p + row + 2) * ROW + 16 + g
            pad[i, pl.ds(start, 16, stride=8), :] = v[p * 16 : p * 16 + 16]

    def spread_activation(i):
        for g in range(8):
            v = jnp.maximum(xb[i, :, g * 128 : g * 128 + 128].astype(F32), 0.0)
            to_pixels(apad, i, g, v)

    def conv(pad, i, which, lo, hi, finish):
        def step(p, _):
            acc = jnp.zeros((16, 8, 128), F32)
            for a in range(5):
                line = pad[i, pl.ds((p + a) * ROW, ROW), :].reshape(20, 8, 128)
                for b in range(5):
                    tap = kkb[i, which, pl.ds((a * 5 + b) * 8, 8), :]
                    acc = acc + line[b : b + 16] * tap[None]
            by_group = jnp.swapaxes(acc, 0, 1)
            here = pl.ds(pl.multiple_of(p * 16, 16), 16)
            for g in range(8):
                finish(here, slice(g * 128, g * 128 + 128), by_group[g])
            return 0

        lax.fori_loop(lo, hi, step, 0)

    def conv_back(pad, i, which, lo, hi, finish):
        taps = []
        for t in range(25):
            tap = kkb[i, which, pl.ds(t * 8, 8), :]
            taps.append(jnp.concatenate([tap, tap], axis=0).astype(BF))

        def step(half, _):
            p = half * 2
            lines = []
            for a in range(6):
                line = pad[i, pl.ds((p + a) * ROW, ROW), :].reshape(20, 8, 128)
                lines.append(jnp.concatenate([line[0:12], line[8:20]], axis=1).astype(BF))
            for r in range(2):
                total = None
                for a in range(5):
                    group = None
                    for b in range(5):
                        term = lines[r + 4 - a][4 - b : 12 - b] * taps[a * 5 + b][None]
                        group = term if group is None else group + term
                    total = group.astype(F32) if total is None else total + group.astype(F32)
                acc = jnp.concatenate([total[:, 0:8], total[:, 8:16]], axis=0)
                by_group = jnp.swapaxes(acc, 0, 1)
                here = pl.ds(pl.multiple_of((p + r) * 16, 16), 16)
                for g in range(8):
                    finish(here, slice(g * 128, g * 128 + 128), by_group[g])
            return 0

        lax.fori_loop(lo // 2, hi // 2, step, 0)

    def rounded_to(ref, i):
        def finish(here, cols, v):
            ref[i, here, cols] = v.astype(BF)

        return finish

    def first_part(i):
        spread_activation(i)
        conv(apad, i, 0, 0, 16, rounded_to(bb, i))

    def second_part(i):
        for n in range(4):
            pre = dot_nn(bb[i], wb[i, 0, :, :, :, :, n * 256 : n * 256 + 256].reshape(CH, 256))
            sg = 1.0 / (1.0 + jnp.exp(-pre))
            slope[i, :, n * 256 : n * 256 + 256] = sg * (1.0 + pre * (1.0 - sg))
            hidden = (pre * sg).astype(BF).astype(F32)
            for g in range(2):
                to_pixels(epad, i, n * 2 + g, hidden[:, g * 128 : g * 128 + 128])

    a1p.wait_recv()
    a1q = push(cell(0, x, y3, 0, 32), 6, up)
    a1m.wait_recv()
    a1n = push(cell(0, x, y1, 32, 32), 7, down)
    b1p.wait_recv()
    b1q = push(cell(1, x3, y, 0, 32), 8, right)
    b1m.wait_recv()
    b1n = push(cell(1, x1, y, 32, 32), 9, left)

    for n, yr in enumerate((y3, y1)):
        a2r.append(push(cell(0, x, yr), 74 + n, right))
        a2l.append(push(cell(0, x, yr), 78 + n, left))
    for n, xr in enumerate((x3, x1)):
        b2u.append(push(cell(1, xr, y), 82 + n, up))
        b2d.append(push(cell(1, xr, y), 86 + n, down))
    a1q.wait_recv()
    a1n.wait_recv()
    a2r.append(push(cell(0, x, y2), 76, right))
    a2l.append(push(cell(0, x, y2), 80, left))
    b1q.wait_recv()
    b1n.wait_recv()
    b2u.append(push(cell(1, x2, y), 84, up))
    b2d.append(push(cell(1, x2, y), 88, down))
    kx.start()
    xx.start()
    fa = [push(xa(x), 14, sibling)]
    fb_ = [push(ybk(y), 15, sibling)]

    first_part(home)

    passed = turn4(x, 1 + 2 * xl)
    onward = at(turn4(x, 3 - 2 * xl), y, z, c)
    a2f, b2f = [], []
    for n, (yr, xr) in enumerate(((y, x), (y3, x3), (y1, x1), (y2, x2))):
        a2r[n].wait_recv()
        a2l[n].wait_recv()
        a2f.append(push(cell(0, passed, yr), 89 + n, onward))
        b2u[n].wait_recv()
        b2f.append(push(cell(1, xr, y3, 0, 32), 93 + n, up))
        b2d[n].wait_recv()
        b2f.append(push(cell(1, xr, y1, 32, 32), 97 + n, down))

    fa.append(push(xa(x3), 20, sibling))
    fb_.append(push(ybk(y3), 22, sibling))
    fb_.append(push(ybk(y1), 23, sibling))
    fa.append(push(xa(x1), 21, sibling))
    for copy in a2f:
        copy.wait_recv()
    fa.append(push(xa(x2), 24, sibling))
    for copy in b2f:
        copy.wait_recv()
    fb_.append(push(ybk(y2), 25, sibling))

    def other_input():
        kx.wait_recv()
        xx.wait_recv()
        first_part(1 - home)

    @pl.when((z < 7) | (xl == 0))
    def _():
        other_input()

    for copy in fa:
        copy.wait_recv()
    second_part(0)

    def third_part(i, _):
        conv(epad, i, 1, 0, 16, rounded_to(fb, i))
        return 0

    @pl.when(z < 7)
    def _():
        second_part(1)
        lax.fori_loop(0, 2, third_part, 0)

    for copy in fb_:
        copy.wait_recv()

    hops = [
        remote(dyb.at[2, pl.ds(k * 64, 64)], dyb.at[0, pl.ds(k * 64, 64)], (26, 54, 55, 56)[k], ahead)
        for k in range(4)
    ]

    @pl.when(z == 7)
    def _():
        load = local(cot_hbm.at[mine], dyb.at[0], 3)
        load.start()
        load.wait()

    def grad_mix(i, lo, n_rows):
        for n in range(4):
            gf = dot_nt(
                dyb[i, pl.ds(lo * 16, n_rows * 16)],
                wb[i, 1, n // 2, pl.ds((n % 2) * 2, 2)].reshape(256, CH),
            )
            for g in range(2):
                to_pixels(gpad, i, n * 2 + g, gf[:, g * 128 : g * 128 + 128], lo)

    def grad_lin(i):
        for n in range(4):
            gl = dot_nt(dcb[i], wb[i, 0, n // 2, pl.ds((n % 2) * 2, 2)].reshape(256, CH))
            for g in range(2):
                to_pixels(bpad, i, n * 2 + g, gl[:, g * 128 : g * 128 + 128])

    def through_slope(i):
        def finish(here, cols, v):
            dcb[i, here, cols] = (v * slope[i, here, cols]).astype(BF)

        return finish

    def onto_input(i):
        def finish(here, cols, v):
            kept = jnp.where(xb[i, here, cols].astype(F32) > 0, v, 0.0)
            dyb[i + 1, here, cols] = (dyb[i, here, cols].astype(F32) + kept).astype(BF)

        return finish

    def weigh(i):
        for n in range(4):
            cols = slice(n * 256, n * 256 + 256)
            first = dot_tn(bb[i, :, cols], dcb[i])
            pb[i, 0, n // 2, pl.ds((n % 2) * 2, 2)] = first.astype(BF).reshape(2, 2, 64, CH)
            second = dot_tn(fb[i, :, cols], dyb[i])
            pb[i, 1, n // 2, pl.ds((n % 2) * 2, 2)] = second.astype(BF).reshape(2, 2, 64, CH)

    def tap_sums(i, which, vpad, tpad):
        def step(p, totals):
            grad = tpad[i, pl.ds((p + 2) * ROW + 16, 128), :].reshape(16, 8, 128)
            out = []
            for a in range(5):
                line = vpad[i, pl.ds((p + a) * ROW, ROW), :].reshape(20, 8, 128)
                for b in range(5):
                    out.append(totals[a * 5 + b] + jnp.sum(line[b : b + 16] * grad, axis=0))
            return tuple(out)

        totals = lax.fori_loop(0, 16, step, tuple(jnp.zeros((8, 128), F32) for _ in range(25)))
        for t in range(25):
            kgf[i, pl.ds(which * 200 + t * 8, 8), :] = totals[t]

    def gya(r, core, lo=0, n=2):
        return pb.at[pl.ds(lo, n), 0, :, r, core]

    def gxb(r, core, lo=0, n=4):
        s, h = place_x(r)
        return pb.at[s, 1, h, pl.ds(lo, n), core]

    def gxa(r, lo=0, n=64):
        s, h = place_x(r)
        return pb.at[s, 0, h, y, c, pl.ds(lo, n)]

    def gyb(r, lo=0, n=64):
        return pb.at[home, 1, xh, r, c, pl.ds(lo, n)]

    def plus(ref, *others):
        total = ref[...].astype(F32)
        for other in others:
            total = total + other[...].astype(F32)
        return total

    pairs = [
        [remote(pb.at[s, h, :, :, 1 - c], r0.at[h, s], 57 + s * 2 + h, sibling) for h in range(2)]
        for s in range(2)
    ]
    d1p = remote(gya(y2, c, 0, 1), ra1.at[0], 31, up)
    d1m = remote(gya(y2, c, 1, 1), ra1.at[1], 32, down)
    e1p = remote(gxb(x2, c, 0, 2), rb1.at[0], 33, right)
    e1m = remote(gxb(x2, c, 2, 2), rb1.at[1], 34, left)
    d2p = [remote(gya(y1, c, 1, 1), ra2.at[0, 1:2], 38, up)]
    d2m = [remote(gya(y3, c, 0, 1), ra2.at[1, 0:1], 39, down)]
    e2p = [remote(gxb(x1, c, 2, 2), rb2.at[0, 2:4], 40, right)]
    e2m = [remote(gxb(x3, c, 0, 2), rb2.at[1, 0:2], 41, left)]
    early = [*pairs[0], *pairs[1], d1p, d1m, e1p, e1m, *d2p, *d2m, *e2p, *e2m]

    def merge(s, which):
        pairs[s][which].wait_recv()

        def step(b, _):
            h, r = lax.div(b, 4), lax.rem(b, 4)
            total = pb[s, which, h, r, c].astype(F32) + r0[which, s, h, r].astype(F32)
            pb[s, which, h, r, c] = total.astype(BF)
            return 0

        lax.fori_loop(0, 8, step, 0)

    def open_section(s):
        weigh(s)
        pairs[s][0].start()
        pairs[s][1].start()

    def send_section(s):
        merge(s, 0)
        (d1p, d1m)[s].start()
        (d2m, d2p)[s][0].start()
        merge(s, 1)

        @pl.when(xl == 1 - s)
        def _():
            e1p.start()
            e1m.start()

        @pl.when(xl == s)
        def _():
            e2p[0].start()
            e2m[0].start()

    done = 0
    for k, ready in enumerate((0, 6, 10, 16)):
        @pl.when(z < 7)
        def _():
            hops[k].wait_recv()

        grad_mix(0, k * 4, 4)
        if ready > done:
            conv_back(gpad, 0, 1, done, ready, through_slope(0))
        done = ready
    grad_lin(0)
    conv_back(bpad, 0, 0, 0, 16, onto_input(0))

    backs = [
        remote(dyb.at[1 + xl, pl.ds(k * 64, 64)], dxr.at[pl.ds(k * 64, 64)], (27, 101, 102, 103)[k], partner)
        for k in range(4)
    ]

    @pl.when(xl == 0)
    def _():
        for copy in backs:
            copy.start()

    @pl.when((z == 7) & (xl == 1))
    def _():
        other_input()

    @pl.when(z == 7)
    def _():
        second_part(1)

    @pl.when(z == 0)
    def _():
        open_section(0)

    grad_mix(1, 0, 16)
    conv_back(gpad, 1, 1, 0, 16, through_slope(1))

    @pl.when(z == 0)
    def _():
        send_section(0)

    grad_lin(1)
    for k in range(4):
        conv_back(bpad, 1, 0, k * 4, k * 4 + 4, onto_input(1))

        @pl.when(z > 0)
        def _():
            if k == 0:
                @pl.when((z == 7) & (c == 1))
                def _():
                    pl.semaphore_wait(turn, 1)

            hops[k].start()

        @pl.when(xl == 1)
        def _():
            backs[k].start()

    @pl.when((z == 7) & (c == 0))
    def _():
        for hop in hops:
            hop.wait_send()
        pl.semaphore_signal(turn, inc=1, device_id=sibling, device_id_type=MESH)

    @pl.when(z == 7)
    def _():
        lax.fori_loop(0, 2, third_part, 0)

    @pl.when(z > 0)
    def _():
        open_section(0)

    open_section(1)

    @pl.when(z > 0)
    def _():
        send_section(0)

    send_section(1)

    def pass_on(first, ref, arrived, dst, k, device):
        first.wait_recv()
        ref[...] = plus(ref, arrived).astype(BF)
        return go(ref, dst, k, device)

    d2p.append(pass_on(d1p, gya(y1, c, 0, 1), ra1.at[0], ra2.at[0, 0:1], 65, up))
    tap_sums(0, 0, apad, bpad)
    e2p.append(pass_on(e1p, gxb(x1, c, 0, 2), rb1.at[0], rb2.at[0, 0:2], 67, right))
    e2m.append(pass_on(e1m, gxb(x3, c, 2, 2), rb1.at[1], rb2.at[1, 2:4], 68, left))
    tap_sums(0, 1, epad, gpad)
    d2m.append(pass_on(d1m, gya(y3, c, 1, 1), ra1.at[1], ra2.at[1, 1:2], 66, down))
    tap_sums(1, 0, apad, bpad)
    tap_sums(1, 1, epad, gpad)
    kgs[...] = kgf[1 - c].astype(BF)
    k0 = go(kgs, kgc, 30, sibling)

    k0.wait_recv()
    kgt[...] = (kgf[c] + kgc[...].astype(F32)).astype(BF)
    ky = [go(kgt, kgy.at[j], 35 + j, device) for j, device in enumerate((up, far_y, down))]

    for copy in d2p + d2m:
        copy.wait_recv()
    gya(y, c)[...] = plus(gya(y, c), ra2.at[0], ra2.at[1]).astype(BF)
    d3p = go(gxa(x2, 0, 32), sa1.at[0], 45, right)
    d3m = go(gxa(x2, 32, 32), sa1.at[1], 46, left)
    d4p = [go(gxa(x1, 32, 32), sa2.at[0, 32:64], 50, right)]
    d4m = [go(gxa(x3, 0, 32), sa2.at[1, 0:32], 51, left)]
    for copy in ky:
        copy.wait_recv()
    kgu[...] = plus(kgt, kgy.at[0], kgy.at[1], kgy.at[2]).astype(BF)
    kq = [go(kgu, kgx.at[j], 42 + j, device) for j, device in enumerate((right, far_x, left))]

    for copy in e2p + e2m:
        copy.wait_recv()
    gxb(x, c)[...] = plus(gxb(x, c), rb2.at[0], rb2.at[1]).astype(BF)
    e3p = go(gyb(y2, 0, 32), sb1.at[0], 47, up)
    e3m = go(gyb(y2, 32, 32), sb1.at[1], 48, down)
    e4p = [go(gyb(y1, 32, 32), sb2.at[0, 32:64], 52, up)]
    e4m = [go(gyb(y3, 0, 32), sb2.at[1, 0:32], 53, down)]

    d4p.append(pass_on(d3p, gxa(x1, 0, 32), sa1.at[0], sa2.at[0, 0:32], 69, right))
    d4m.append(pass_on(d3m, gxa(x3, 32, 32), sa1.at[1], sa2.at[1, 32:64], 70, left))
    e4p.append(pass_on(e3p, gyb(y1, 0, 32), sb1.at[0], sb2.at[0, 0:32], 71, up))
    e4m.append(pass_on(e3m, gyb(y3, 32, 32), sb1.at[1], sb2.at[1, 32:64], 72, down))

    for copy in backs:
        copy.wait_recv()
    store0 = local(dyb.at[home + 1], dx_out.at[mine], 4)
    store1 = local(dxr, dx_out.at[1 - mine], 5)
    store0.start()
    store1.start()

    for copy in d4p + d4m:
        copy.wait_recv()
    gp_out[0] = plus(gxa(x), sa2.at[0], sa2.at[1]) * SCALE
    for copy in e4p + e4m:
        copy.wait_recv()
    gp_out[1] = plus(gyb(y), sb2.at[0], sb2.at[1]) * SCALE

    for copy in kq:
        copy.wait_recv()
    kgv[...] = plus(kgu, kgx.at[0], kgx.at[1], kgx.at[2]).astype(BF)
    k3 = go(kgv, kgw, 49, sibling)
    k3.wait_recv()
    own = (c == home).astype(F32)
    gd_out[...] = (kgv[...].astype(F32) * own + kgw[...].astype(F32) * (1.0 - own)) * SCALE

    store0.wait()
    store1.wait()
    for copy in sent + backs + early + [kx, xx]:
        copy.wait_send()

    @pl.when((z > 0) & ((z < 7) | (c == 1)))
    def _():
        for hop in hops:
            hop.wait_send()


def body(checkpoint, cotangent, depthwise, pointwise, genotype):
    x = checkpoint.reshape(2, PIX, CH)
    cot = cotangent.reshape(2, PIX, CH)
    keep = tap_mask(genotype[0])
    kk = (depthwise[0] * keep[None, :, None]).reshape(2, 200, 128)
    w = jnp.transpose(pointwise[0], (1, 0, 2))
    anywhere = pl.BlockSpec(memory_space=pl.ANY)
    here = pl.BlockSpec(memory_space=pltpu.VMEM)
    pad = pltpu.VMEM((2, PADDED, 128), F32)
    taps = pltpu.VMEM((400, 128), BF)
    image2 = pltpu.VMEM((2, PIX, CH), BF)
    dx, gp, gd = pl.pallas_call(
        kernel,
        out_shape=(
            jax.ShapeDtypeStruct((2, PIX, CH), BF),
            jax.ShapeDtypeStruct((2, 64, CH), F32),
            jax.ShapeDtypeStruct((400, 128), F32),
        ),
        in_specs=[anywhere] * 4,
        out_specs=(anywhere, here, here),
        scratch_shapes=[
            pltpu.VMEM((2, 2, 2, 4, 2, 64, CH), BF),
            pltpu.VMEM((2, 2, 2, 4, 2, 64, CH), BF),
            image2,
            pltpu.VMEM((2, 2, 200, 128), F32),
            pad, pad, pad, pad,
            pltpu.VMEM((2, PIX, CH), F32),
            image2, image2, image2,
            pltpu.VMEM((3, PIX, CH), BF),
            pltpu.VMEM((PIX, CH), BF),
            pltpu.VMEM((2, 2, 2, 4, 64, CH), BF),
            pltpu.VMEM((2, 1, 2, 64, CH), BF),
            pltpu.VMEM((2, 2, 2, 64, CH), BF),
            pltpu.VMEM((2, 32, CH), BF),
            pltpu.VMEM((2, 64, CH), BF),
            pltpu.VMEM((2, 2, 64, CH), BF),
            pltpu.VMEM((2, 4, 64, CH), BF),
            pltpu.VMEM((2, 32, CH), BF),
            pltpu.VMEM((2, 64, CH), BF),
            pltpu.VMEM((2, 400, 128), F32),
            taps, taps, taps,
            pltpu.VMEM((3, 400, 128), BF),
            taps,
            pltpu.VMEM((3, 400, 128), BF),
            taps, taps,
            pltpu.SemaphoreType.DMA((6,)),
            pltpu.SemaphoreType.DMA((104,)),
            pltpu.SemaphoreType.DMA((104,)),
            pltpu.SemaphoreType.REGULAR,
        ],
        compiler_params=pltpu.CompilerParams(
            collective_id=0, has_side_effects=True, vmem_limit_bytes=66_000_000
        ),
    )(x, cot, w, kk)
    grad_depth = gd.reshape(2, 25, CH) * keep[None, :, None]
    return (
        dx.reshape(checkpoint.shape),
        jnp.transpose(gp, (1, 0, 2))[None],
        grad_depth[None],
    )


def solution(mesh):
    placed = (
        P("segment", None, "dp", None, None, None),
        P(None, "dp", None, None, None),
        P("segment", None, None, None),
        P("segment", "dp", None, None),
        P("segment"),
    )
    return jax.shard_map(
        body,
        mesh=mesh,
        in_specs=placed,
        out_specs=(
            P("segment", None, "dp", None, None, None),
            P("segment", "dp", None, None),
            P("segment", None, None, None),
        ),
        check_vma=False,
    )
```

```python
import jax
import jax.numpy as jnp
from jax import lax
from jax.experimental import pallas as pl
from jax.experimental.pallas import tpu as pltpu
from jax.sharding import PartitionSpec as P

BF = jnp.bfloat16
F32 = jnp.float32
MESH = pl.DeviceIdType.MESH
PIX = 256
CH = 1024
ROW = 160
PADDED = 20 * ROW
SCALE = 1.0 / 32


def tap_mask(operation):
    tap_ids = jnp.arange(25, dtype=jnp.int32)
    row_off = tap_ids // 5 - 2
    col_off = tap_ids % 5 - 2
    narrow = (jnp.abs(row_off) <= 1) & (jnp.abs(col_off) <= 1)
    dilated = (row_off % 2 == 0) & (col_off % 2 == 0)
    kept_taps = jnp.where(operation == 0, narrow, jnp.where(operation == 1, True, dilated))
    return kept_taps.astype(F32)


def dot_nn(a, b):
    return lax.dot_general(a, b, (((1,), (0,)), ((), ())), preferred_element_type=F32)


def dot_nt(a, b):
    return lax.dot_general(a, b, (((1,), (1,)), ((), ())), preferred_element_type=F32)


def dot_tn(a, b):
    return lax.dot_general(a, b, (((0,), (0,)), ((), ())), preferred_element_type=F32)


def kernel(
    x_hbm, cot_hbm, w_hbm, kk_hbm,
    dx_out, gp_out, gd_out,
    wb, pb, xb, kkb, apad, epad, gpad, bpad, slope, bb, fb, dcb, dyb, dxr,
    r0, ra1, ra2, sa1, sa2, rb1, rb2, sb1, sb2,
    kgf, kgs, kgc, kgt, kgy, kgu, kgx, kgv, kgw,
    ls, ss, rs, turn,
):
    seg = lax.axis_index("segment")
    dp = lax.axis_index("dp")
    z, xl = lax.div(seg, 2), lax.rem(seg, 2)
    xh, y, c = lax.div(dp, 8), lax.rem(lax.div(dp, 2), 4), lax.rem(dp, 2)
    x = xh * 2 + xl
    home = 1 - xl
    mine = 1 - xl

    def at(x_, y_, z_, c_):
        return (z_ * 2 + lax.rem(x_, 2), lax.div(x_, 2) * 8 + y_ * 2 + c_)

    def turn4(v, by):
        return lax.rem(v + by, 4)

    x1, x2, x3 = turn4(x, 1), turn4(x, 2), turn4(x, 3)
    y1, y2, y3 = turn4(y, 1), turn4(y, 2), turn4(y, 3)
    right, far_x, left = at(x1, y, z, c), at(x2, y, z, c), at(x3, y, z, c)
    up, far_y, down = at(x, y1, z, c), at(x, y2, z, c), at(x, y3, z, c)
    sibling = at(x, y, z, 1 - c)
    partner = at(xh * 2 + 1 - xl, y, z, c)
    ahead = at(x, y, lax.rem(z + 7, 8), c)
    behind = at(x, y, lax.rem(z + 1, 8), c)

    def remote(src, dst, k, device):
        return pltpu.make_async_remote_copy(
            src_ref=src, dst_ref=dst, send_sem=ss.at[k], recv_sem=rs.at[k],
            device_id=device, device_id_type=MESH,
        )

    def local(src, dst, k):
        return pltpu.make_async_copy(src, dst, ls.at[k])

    barrier = pltpu.get_barrier_semaphore()
    greeted = (right, far_x, left, up, far_y, down, sibling, ahead, behind)
    for device in greeted:
        pl.semaphore_signal(barrier, inc=1, device_id=device, device_id_type=MESH)

    loads = [
        local(w_hbm, wb.at[home, :, xh, y, c], 0),
        local(x_hbm.at[mine], xb.at[home], 1),
        local(kk_hbm, kkb.at[home], 2),
    ]
    for load in loads:
        load.start()

    @pl.loop(0, 20)
    def _(r):
        nothing = jnp.zeros((ROW, 128), F32)
        for pad in (apad, epad, gpad, bpad):
            for i in range(2):
                pad[i, pl.ds(r * ROW, ROW), :] = nothing

    pl.semaphore_wait(barrier, len(greeted))

    for load in loads:
        load.wait()
    sent = []

    def go(src, dst, k, device):
        copy = remote(src, dst, k, device)
        copy.start()
        sent.append(copy)
        return copy

    def place_x(r):
        return 1 - lax.rem(r, 2), lax.div(r, 2)

    def cell(which, xr, yr, lo=0, n=64):
        s, h = place_x(xr)
        return wb.at[s, which, h, yr, c, pl.ds(lo, n)]

    def xa(r):
        s, h = place_x(r)
        return wb.at[s, 0, h, :, c]

    def ybk(r):
        return wb.at[:, 1, :, r, c]

    def push(ref, k, device):
        return go(ref, ref, k, device)

    a1p = push(cell(0, x, y), 0, up)
    a1m = push(cell(0, x, y), 1, down)
    b1p = push(cell(1, x, y), 2, right)
    b1m = push(cell(1, x, y), 3, left)
    a2r = [push(cell(0, x, y), 73, right)]
    a2l = [push(cell(0, x, y), 77, left)]
    b2u = [push(cell(1, x, y), 81, up)]
    b2d = [push(cell(1, x, y), 85, down)]
    kx = remote(kk_hbm, kkb.at[home], 4, partner)
    xx = remote(x_hbm.at[xl], xb.at[home], 5, partner)

    def to_pixels(pad, i, g, v, row=0):
        for p in range(v.shape[0] // 16):
            start = (p + row + 2) * ROW + 16 + g
            pad[i, pl.ds(start, 16, stride=8), :] = v[p * 16 : p * 16 + 16]

    def spread_activation(i):
        for g in range(8):
            v = jnp.maximum(xb[i, :, g * 128 : g * 128 + 128].astype(F32), 0.0)
            to_pixels(apad, i, g, v)

    def conv(pad, i, which, lo, hi, finish):
        def step(p, _):
            acc = jnp.zeros((16, 8, 128), F32)
            for a in range(5):
                line = pad[i, pl.ds((p + a) * ROW, ROW), :].reshape(20, 8, 128)
                for b in range(5):
                    tap = kkb[i, which, pl.ds((a * 5 + b) * 8, 8), :]
                    acc = acc + line[b : b + 16] * tap[None]
            by_group = jnp.swapaxes(acc, 0, 1)
            here = pl.ds(pl.multiple_of(p * 16, 16), 16)
            for g in range(8):
                finish(here, slice(g * 128, g * 128 + 128), by_group[g])
            return 0

        lax.fori_loop(lo, hi, step, 0)

    def conv_bf16(pad, i, which, flip, lo, hi, finish):
        taps = []
        for t in range(25):
            tap = kkb[i, which, pl.ds(t * 8, 8), :]
            taps.append(jnp.concatenate([tap, tap], axis=0).astype(BF))

        def step(half, _):
            p = half * 2
            lines = []
            for a in range(6):
                line = pad[i, pl.ds((p + a) * ROW, ROW), :].reshape(20, 8, 128)
                lines.append(jnp.concatenate([line[0:12], line[8:20]], axis=1).astype(BF))
            for r in range(2):
                total = None
                for rows in ((0, 1), (2, 3), (4,)):
                    group = None
                    for a in rows:
                        for b in range(5):
                            p_off, q = (4 - a, 4 - b) if flip else (a, b)
                            term = lines[r + p_off][q : q + 8] * taps[a * 5 + b][None]
                            group = term if group is None else group + term
                    total = group.astype(F32) if total is None else total + group.astype(F32)
                acc = jnp.concatenate([total[:, 0:8], total[:, 8:16]], axis=0)
                by_group = jnp.swapaxes(acc, 0, 1)
                here = pl.ds(pl.multiple_of((p + r) * 16, 16), 16)
                for g in range(8):
                    finish(here, slice(g * 128, g * 128 + 128), by_group[g])
            return 0

        lax.fori_loop(lo // 2, hi // 2, step, 0)

    def rounded_to(ref, i):
        def finish(here, cols, v):
            ref[i, here, cols] = v.astype(BF)

        return finish

    def first_part(i):
        spread_activation(i)
        conv_bf16(apad, i, 0, False, 0, 16, rounded_to(bb, i))

    def second_part(i):
        for n in range(4):
            pre = dot_nn(bb[i], wb[i, 0, :, :, :, :, n * 256 : n * 256 + 256].reshape(CH, 256))
            sg = 1.0 / (1.0 + jnp.exp(-pre))
            slope[i, :, n * 256 : n * 256 + 256] = sg * (1.0 + pre * (1.0 - sg))
            hidden = (pre * sg).astype(BF).astype(F32)
            for g in range(2):
                to_pixels(epad, i, n * 2 + g, hidden[:, g * 128 : g * 128 + 128])

    a1p.wait_recv()
    a1q = push(cell(0, x, y3, 0, 32), 6, up)
    a1m.wait_recv()
    a1n = push(cell(0, x, y1, 32, 32), 7, down)
    b1p.wait_recv()
    b1q = push(cell(1, x3, y, 0, 32), 8, right)
    b1m.wait_recv()
    b1n = push(cell(1, x1, y, 32, 32), 9, left)

    for n, yr in enumerate((y3, y1)):
        a2r.append(push(cell(0, x, yr), 74 + n, right))
        a2l.append(push(cell(0, x, yr), 78 + n, left))
    for n, xr in enumerate((x3, x1)):
        b2u.append(push(cell(1, xr, y), 82 + n, up))
        b2d.append(push(cell(1, xr, y), 86 + n, down))
    a1q.wait_recv()
    a1n.wait_recv()
    a2r.append(push(cell(0, x, y2), 76, right))
    a2l.append(push(cell(0, x, y2), 80, left))
    b1q.wait_recv()
    b1n.wait_recv()
    b2u.append(push(cell(1, x2, y), 84, up))
    b2d.append(push(cell(1, x2, y), 88, down))
    kx.start()
    xx.start()
    fa = [push(xa(x), 14, sibling)]
    fb_ = [push(ybk(y), 15, sibling)]

    first_part(home)

    passed = turn4(x, 1 + 2 * xl)
    onward = at(turn4(x, 3 - 2 * xl), y, z, c)
    a2f, b2f = [], []
    for n, (yr, xr) in enumerate(((y, x), (y3, x3), (y1, x1), (y2, x2))):
        a2r[n].wait_recv()
        a2l[n].wait_recv()
        a2f.append(push(cell(0, passed, yr), 89 + n, onward))
        b2u[n].wait_recv()
        b2f.append(push(cell(1, xr, y3, 0, 32), 93 + n, up))
        b2d[n].wait_recv()
        b2f.append(push(cell(1, xr, y1, 32, 32), 97 + n, down))

    fa.append(push(xa(x3), 20, sibling))
    fb_.append(push(ybk(y3), 22, sibling))
    fb_.append(push(ybk(y1), 23, sibling))
    fa.append(push(xa(x1), 21, sibling))
    for copy in a2f:
        copy.wait_recv()
    fa.append(push(xa(x2), 24, sibling))
    for copy in b2f:
        copy.wait_recv()
    fb_.append(push(ybk(y2), 25, sibling))

    def other_input():
        kx.wait_recv()
        xx.wait_recv()
        first_part(1 - home)

    @pl.when((z < 7) | (xl == 0))
    def _():
        other_input()

    for copy in fa:
        copy.wait_recv()
    second_part(0)

    def third_part(i, _):
        conv(epad, i, 1, 0, 16, rounded_to(fb, i))
        return 0

    @pl.when(z < 7)
    def _():
        second_part(1)
        lax.fori_loop(0, 2, third_part, 0)

    for copy in fb_:
        copy.wait_recv()

    hops = [
        remote(dyb.at[2, pl.ds(k * 64, 64)], dyb.at[0, pl.ds(k * 64, 64)], (26, 54, 55, 56)[k], ahead)
        for k in range(4)
    ]

    @pl.when(z == 7)
    def _():
        load = local(cot_hbm.at[mine], dyb.at[0], 3)
        load.start()
        load.wait()

    def grad_mix(i, lo, n_rows):
        for n in range(4):
            gf = dot_nt(
                dyb[i, pl.ds(lo * 16, n_rows * 16)],
                wb[i, 1, n // 2, pl.ds((n % 2) * 2, 2)].reshape(256, CH),
            )
            for g in range(2):
                to_pixels(gpad, i, n * 2 + g, gf[:, g * 128 : g * 128 + 128], lo)

    def grad_lin(i):
        for n in range(4):
            gl = dot_nt(dcb[i], wb[i, 0, n // 2, pl.ds((n % 2) * 2, 2)].reshape(256, CH))
            for g in range(2):
                to_pixels(bpad, i, n * 2 + g, gl[:, g * 128 : g * 128 + 128])

    def through_slope(i):
        def finish(here, cols, v):
            dcb[i, here, cols] = (v * slope[i, here, cols]).astype(BF)

        return finish

    def onto_input(i):
        def finish(here, cols, v):
            kept = jnp.where(xb[i, here, cols].astype(F32) > 0, v, 0.0)
            dyb[i + 1, here, cols] = (dyb[i, here, cols].astype(F32) + kept).astype(BF)

        return finish

    done = 0
    for k, ready in enumerate((0, 6, 10, 16)):
        @pl.when(z < 7)
        def _():
            hops[k].wait_recv()

        grad_mix(0, k * 4, 4)
        if ready > done:
            conv_bf16(gpad, 0, 1, True, done, ready, through_slope(0))
        done = ready
    grad_lin(0)
    conv_bf16(bpad, 0, 0, True, 0, 16, onto_input(0))

    backs = [
        remote(dyb.at[1 + xl, pl.ds(k * 64, 64)], dxr.at[pl.ds(k * 64, 64)], (27, 101, 102, 103)[k], partner)
        for k in range(4)
    ]

    @pl.when(xl == 0)
    def _():
        for copy in backs:
            copy.start()

    @pl.when((z == 7) & (xl == 1))
    def _():
        other_input()

    @pl.when(z == 7)
    def _():
        second_part(1)

    grad_mix(1, 0, 16)
    conv_bf16(gpad, 1, 1, True, 0, 16, through_slope(1))
    grad_lin(1)
    for k in range(4):
        conv_bf16(bpad, 1, 0, True, k * 4, k * 4 + 4, onto_input(1))

        @pl.when(z > 0)
        def _():
            if k == 0:
                @pl.when((z == 7) & (c == 1))
                def _():
                    pl.semaphore_wait(turn, 1)

            hops[k].start()

        @pl.when(xl == 1)
        def _():
            backs[k].start()

    @pl.when((z == 7) & (c == 0))
    def _():
        for hop in hops:
            hop.wait_send()
        pl.semaphore_signal(turn, inc=1, device_id=sibling, device_id_type=MESH)

    @pl.when(z == 7)
    def _():
        lax.fori_loop(0, 2, third_part, 0)

    def weigh(i, _):
        for n in range(4):
            cols = slice(n * 256, n * 256 + 256)
            first = dot_tn(bb[i, :, cols], dcb[i])
            pb[i, 0, n // 2, pl.ds((n % 2) * 2, 2)] = first.astype(BF).reshape(2, 2, 64, CH)
            second = dot_tn(fb[i, :, cols], dyb[i])
            pb[i, 1, n // 2, pl.ds((n % 2) * 2, 2)] = second.astype(BF).reshape(2, 2, 64, CH)
        return 0

    lax.fori_loop(0, 2, weigh, 0)

    def tap_sums(i, which, vpad, tpad):
        def step(p, totals):
            grad = tpad[i, pl.ds((p + 2) * ROW + 16, 128), :].reshape(16, 8, 128)
            out = []
            for a in range(5):
                line = vpad[i, pl.ds((p + a) * ROW, ROW), :].reshape(20, 8, 128)
                for b in range(5):
                    out.append(totals[a * 5 + b] + jnp.sum(line[b : b + 16] * grad, axis=0))
            return tuple(out)

        totals = lax.fori_loop(0, 16, step, tuple(jnp.zeros((8, 128), F32) for _ in range(25)))
        for t in range(25):
            kgf[i, pl.ds(which * 200 + t * 8, 8), :] = totals[t]

    def gya(r, core, lo=0, n=2):
        return pb.at[pl.ds(lo, n), 0, :, r, core]

    def gxb(r, core, lo=0, n=4):
        s, h = place_x(r)
        return pb.at[s, 1, h, pl.ds(lo, n), core]

    def gxa(r, lo=0, n=64):
        s, h = place_x(r)
        return pb.at[s, 0, h, y, c, pl.ds(lo, n)]

    def gyb(r, lo=0, n=64):
        return pb.at[home, 1, xh, r, c, pl.ds(lo, n)]

    def r0a(r):
        return r0.at[0, :, :, r]

    def r0b(r):
        s, h = place_x(r)
        return r0.at[1, s, h]

    def plus(ref, *others):
        total = ref[...].astype(F32)
        for other in others:
            total = total + other[...].astype(F32)
        return total

    pair_a = {}
    pair_b = {}
    for n, (ry, rx) in enumerate(((y2, x2), (y1, x1), (y3, x3), (y, x))):
        pair_a[n] = go(gya(ry, 1 - c), r0a(ry), 57 + n, sibling)
        pair_b[n] = go(gxb(rx, 1 - c), r0b(rx), 61 + n, sibling)

    def merge_a(n, r):
        pair_a[n].wait_recv()
        ref = gya(r, c)
        ref[...] = plus(ref, r0a(r)).astype(BF)

    def merge_b(n, r):
        pair_b[n].wait_recv()
        ref = gxb(r, c)
        ref[...] = plus(ref, r0b(r)).astype(BF)

    merge_a(0, y2)
    d1p = go(gya(y2, c, 0, 1), ra1.at[0], 31, up)
    d1m = go(gya(y2, c, 1, 1), ra1.at[1], 32, down)
    merge_b(0, x2)
    e1p = go(gxb(x2, c, 0, 2), rb1.at[0], 33, right)
    e1m = go(gxb(x2, c, 2, 2), rb1.at[1], 34, left)
    merge_a(1, y1)
    d2p = [go(gya(y1, c, 1, 1), ra2.at[0, 1:2], 38, up)]
    merge_a(2, y3)
    d2m = [go(gya(y3, c, 0, 1), ra2.at[1, 0:1], 39, down)]
    merge_b(1, x1)
    e2p = [go(gxb(x1, c, 2, 2), rb2.at[0, 2:4], 40, right)]
    merge_b(2, x3)
    e2m = [go(gxb(x3, c, 0, 2), rb2.at[1, 0:2], 41, left)]
    tap_sums(0, 0, apad, bpad)
    tap_sums(0, 1, epad, gpad)

    def pass_on(first, ref, arrived, dst, k, device):
        first.wait_recv()
        ref[...] = plus(ref, arrived).astype(BF)
        return go(ref, dst, k, device)

    d2p.append(pass_on(d1p, gya(y1, c, 0, 1), ra1.at[0], ra2.at[0, 0:1], 65, up))
    d2m.append(pass_on(d1m, gya(y3, c, 1, 1), ra1.at[1], ra2.at[1, 1:2], 66, down))
    e2p.append(pass_on(e1p, gxb(x1, c, 0, 2), rb1.at[0], rb2.at[0, 0:2], 67, right))
    e2m.append(pass_on(e1m, gxb(x3, c, 2, 2), rb1.at[1], rb2.at[1, 2:4], 68, left))
    merge_a(3, y)
    merge_b(3, x)
    tap_sums(1, 0, apad, bpad)
    tap_sums(1, 1, epad, gpad)
    kgs[...] = kgf[1 - c].astype(BF)
    k0 = go(kgs, kgc, 30, sibling)

    k0.wait_recv()
    kgt[...] = (kgf[c] + kgc[...].astype(F32)).astype(BF)
    ky = [go(kgt, kgy.at[j], 35 + j, device) for j, device in enumerate((up, far_y, down))]

    for copy in d2p + d2m:
        copy.wait_recv()
    gya(y, c)[...] = plus(gya(y, c), ra2.at[0], ra2.at[1]).astype(BF)
    d3p = go(gxa(x2, 0, 32), sa1.at[0], 45, right)
    d3m = go(gxa(x2, 32, 32), sa1.at[1], 46, left)
    d4p = [go(gxa(x1, 32, 32), sa2.at[0, 32:64], 50, right)]
    d4m = [go(gxa(x3, 0, 32), sa2.at[1, 0:32], 51, left)]
    for copy in ky:
        copy.wait_recv()
    kgu[...] = plus(kgt, kgy.at[0], kgy.at[1], kgy.at[2]).astype(BF)
    kq = [go(kgu, kgx.at[j], 42 + j, device) for j, device in enumerate((right, far_x, left))]

    for copy in e2p + e2m:
        copy.wait_recv()
    gxb(x, c)[...] = plus(gxb(x, c), rb2.at[0], rb2.at[1]).astype(BF)
    e3p = go(gyb(y2, 0, 32), sb1.at[0], 47, up)
    e3m = go(gyb(y2, 32, 32), sb1.at[1], 48, down)
    e4p = [go(gyb(y1, 32, 32), sb2.at[0, 32:64], 52, up)]
    e4m = [go(gyb(y3, 0, 32), sb2.at[1, 0:32], 53, down)]

    d4p.append(pass_on(d3p, gxa(x1, 0, 32), sa1.at[0], sa2.at[0, 0:32], 69, right))
    d4m.append(pass_on(d3m, gxa(x3, 32, 32), sa1.at[1], sa2.at[1, 32:64], 70, left))
    e4p.append(pass_on(e3p, gyb(y1, 0, 32), sb1.at[0], sb2.at[0, 0:32], 71, up))
    e4m.append(pass_on(e3m, gyb(y3, 32, 32), sb1.at[1], sb2.at[1, 32:64], 72, down))

    for copy in backs:
        copy.wait_recv()
    store0 = local(dyb.at[home + 1], dx_out.at[mine], 4)
    store1 = local(dxr, dx_out.at[1 - mine], 5)
    store0.start()
    store1.start()

    for copy in d4p + d4m:
        copy.wait_recv()
    gp_out[:, 0, :] = plus(gxa(x), sa2.at[0], sa2.at[1]) * SCALE
    for copy in e4p + e4m:
        copy.wait_recv()
    gp_out[:, 1, :] = plus(gyb(y), sb2.at[0], sb2.at[1]) * SCALE

    for copy in kq:
        copy.wait_recv()
    kgv[...] = plus(kgu, kgx.at[0], kgx.at[1], kgx.at[2]).astype(BF)
    k3 = go(kgv, kgw, 49, sibling)
    k3.wait_recv()
    own = (c == home).astype(F32)
    gd_out[...] = (kgv[...].astype(F32) * own + kgw[...].astype(F32) * (1.0 - own)) * SCALE

    store0.wait()
    store1.wait()
    for copy in sent + backs + [kx, xx]:
        copy.wait_send()

    @pl.when((z > 0) & ((z < 7) | (c == 1)))
    def _():
        for hop in hops:
            hop.wait_send()


def body(checkpoint, cotangent, depthwise, pointwise, genotype):
    x = checkpoint.reshape(2, PIX, CH)
    cot = cotangent.reshape(2, PIX, CH)
    keep = tap_mask(genotype[0])
    kk = (depthwise[0] * keep[None, :, None]).reshape(2, 200, 128)
    w = jnp.transpose(pointwise[0], (1, 0, 2))
    anywhere = pl.BlockSpec(memory_space=pl.ANY)
    here = pl.BlockSpec(memory_space=pltpu.VMEM)
    pad = pltpu.VMEM((2, PADDED, 128), F32)
    taps = pltpu.VMEM((400, 128), BF)
    image2 = pltpu.VMEM((2, PIX, CH), BF)
    dx, gp, gd = pl.pallas_call(
        kernel,
        out_shape=(
            jax.ShapeDtypeStruct((2, PIX, CH), BF),
            jax.ShapeDtypeStruct((64, 2, CH), F32),
            jax.ShapeDtypeStruct((400, 128), F32),
        ),
        in_specs=[anywhere] * 4,
        out_specs=(anywhere, here, here),
        scratch_shapes=[
            pltpu.VMEM((2, 2, 2, 4, 2, 64, CH), BF),
            pltpu.VMEM((2, 2, 2, 4, 2, 64, CH), BF),
            image2,
            pltpu.VMEM((2, 2, 200, 128), F32),
            pad, pad, pad, pad,
            pltpu.VMEM((2, PIX, CH), F32),
            image2, image2, image2,
            pltpu.VMEM((3, PIX, CH), BF),
            pltpu.VMEM((PIX, CH), BF),
            pltpu.VMEM((2, 2, 2, 4, 64, CH), BF),
            pltpu.VMEM((2, 1, 2, 64, CH), BF),
            pltpu.VMEM((2, 2, 2, 64, CH), BF),
            pltpu.VMEM((2, 32, CH), BF),
            pltpu.VMEM((2, 64, CH), BF),
            pltpu.VMEM((2, 2, 64, CH), BF),
            pltpu.VMEM((2, 4, 64, CH), BF),
            pltpu.VMEM((2, 32, CH), BF),
            pltpu.VMEM((2, 64, CH), BF),
            pltpu.VMEM((2, 400, 128), F32),
            taps, taps, taps,
            pltpu.VMEM((3, 400, 128), BF),
            taps,
            pltpu.VMEM((3, 400, 128), BF),
            taps, taps,
            pltpu.SemaphoreType.DMA((6,)),
            pltpu.SemaphoreType.DMA((104,)),
            pltpu.SemaphoreType.DMA((104,)),
            pltpu.SemaphoreType.REGULAR,
        ],
        compiler_params=pltpu.CompilerParams(
            collective_id=0, has_side_effects=True, vmem_limit_bytes=66_000_000
        ),
    )(x, cot, w, kk)
    grad_depth = gd.reshape(2, 25, CH) * keep[None, :, None]
    return (
        dx.reshape(checkpoint.shape),
        gp[None],
        grad_depth[None],
    )


def solution(mesh):
    placed = (
        P("segment", None, "dp", None, None, None),
        P(None, "dp", None, None, None),
        P("segment", None, None, None),
        P("segment", "dp", None, None),
        P("segment"),
    )
    return jax.shard_map(
        body,
        mesh=mesh,
        in_specs=placed,
        out_specs=(
            P("segment", None, "dp", None, None, None),
            P("segment", "dp", None, None),
            P("segment", None, None, None),
        ),
        check_vma=False,
    )
```
